256 devices in a mesh: row: 16 (over x, y_lo, core), col: 8 (over z), grp: 2 (over y_hi).
Axes of the slice: x: 4, y: 4 (y_hi: 2, y_lo: 2; y = y_hi * 2 + y_lo), z: 8, core: 2. Of those that a mesh axis runs over, the one named last changes fastest.
Arguments:
- patches: bfloat16 [2, 1024, 1408], P('grp', 'row', 'col'), may hold values from -6 to 6
- vis_gain: bfloat16 [1408], P('col'), may hold values from 0.25 to 1.75
- vis_bias: bfloat16 [1408], P('col'), may hold values from -3 to 3
- vis_qkv: bfloat16 [1408, 4224], P('col', 'row'), may hold values from -1 to 1
- vis_qkv_bias: bfloat16 [4224], P('row'), may hold values from -3 to 3
- vis_out: bfloat16 [1408, 1408], P('row', 'col'), may hold values from -0.15625 to 0.15625
- vis_out_bias: bfloat16 [1408], P('col'), may hold values from -3 to 3
- proj_weight: bfloat16 [4, 1408, 1408], P(None, 'col', 'row'), may hold values from -0.078125 to 0.078125
- proj_bias: bfloat16 [1408], P('row'), may hold values from -3 to 3
- text_embeds: bfloat16 [2, 4096, 1408], P('grp', 'col', 'row'), may hold values from -6 to 6
- dec_gain: bfloat16 [1408], P('row'), may hold values from 0.25 to 1.75
- dec_qkv: bfloat16 [1408, 4224], P('row', 'col'), may hold values from -1 to 1
- dec_out: bfloat16 [1408, 1408], P('col', 'row'), may hold values from -0.15625 to 0.15625
- image_tokens: int32 [2, 8], P('grp'), may hold values from 1 to 64, 256 in all within a row
- text_gaps: int32 [2, 9], P('grp'), may hold values from 1 to 1920, 3840 in all within a row
- doc_lengths: int32 [4], replicated, may hold values from 1 to 4096, 8192 in all
Outputs:
- hidden_out: bfloat16 [2, 4096, 1408], P('grp', 'col', 'row')
The draws below stay inside these ranges and needn't reach their ends.
All inputs are finite; a program needn't handle non-finite values.
Results may differ from the reference program's by a relative error of at most 0.0045.
The reference program's roundings to bfloat16 on the way count: a program that leaves them out, or rounds other values in their place, can miss the bound.
Values may be sent and summed in bfloat16 or wider, within the bound.
No kernel may reach another device: no remote copies, remote signals or barrier semaphores. Data moves between devices by JAX's collectives and lax.ppermute only.
A program may use at most 64 MiB of HBM per device.

```python
import math
import jax
import jax.numpy as jnp
import numpy as np
from jax import lax

HEADS = 16
HEAD_DIM = 88
D = 1408
TPD = 256
IMGS = 8
SEGS = 4
HALVES = 2
PH = 1024
MH = 256
SH = 4096


def paired_tokens(key, shape):
    base = jnp.clip(jax.random.normal(jax.random.fold_in(key, 1), shape, jnp.float32), -6.0, 6.0)
    return base.astype(jnp.bfloat16)


def drawn_projection(key):
    factor = D ** (-0.5)
    base = jnp.clip(jax.random.normal(jax.random.fold_in(key, 3), (D, HEADS, 3, HEAD_DIM), jnp.float32), -5.0, 5.0) * factor
    return base.reshape(D, 3 * D).astype(jnp.bfloat16)


def draw_patches(key, part):
    return paired_tokens(jax.random.fold_in(key, 41), (HALVES, PH, D))


def draw_text_embeds(key, part):
    return paired_tokens(jax.random.fold_in(key, 43), (HALVES, SH, D))


def draw_vis_qkv(key, part):
    return drawn_projection(jax.random.fold_in(key, 31))


def draw_dec_qkv(key, part):
    return drawn_projection(jax.random.fold_in(key, 37))


def shard_levels(own_key, dims, split, smallest, top_value):
    loudness = 1.0
    for axis_at, shards_of in split:
        steps = jax.random.uniform(jax.random.fold_in(jax.random.fold_in(own_key, 6), axis_at), (shards_of,), jnp.float32, smallest / len(split), top_value / len(split))
        loudness = loudness * jnp.repeat(jnp.exp(steps), dims[axis_at] // shards_of).reshape((-1,) + (1,) * (len(dims) - 1 - axis_at))
    return loudness


def profile(number_of, total, reach, lean):
    portions = [(1 << 20) // math.isqrt(rank ** lean) + 1 for rank in range(2, number_of + 1)]
    rest, holding = total - reach - (number_of - 1), [1] * (number_of - 1)
    while rest > 0:
        candidates = [i for i in range(number_of - 1) if holding[i] < reach]
        mass, remaining = sum([portions[i] for i in candidates]), rest
        for i in candidates:
            extra = min(reach - holding[i], max(1, remaining * portions[i] // mass), rest)
            holding[i] = holding[i] + extra
            rest = rest - extra
    return np.array([reach] + holding)


def ragged_sizes(rng, number_of, total, limit, lean):
    if number_of == 2:
        one = jax.random.randint(rng, (), max(1, total - limit), min(limit, total - 1) + 1)
        return jnp.stack([one, total - one])
    tallies = jnp.asarray(profile(number_of, total, limit, lean), jnp.int32)
    twos = (number_of - 1) // 2
    donor, receiver = tallies[1:1 + 2 * twos:2], tallies[2:2 + 2 * twos:2]
    room = jnp.minimum(donor - 1, limit - receiver)
    shifted = jax.random.randint(jax.random.fold_in(rng, 1), (twos,), 0, 1 << 20) % (room + 1)
    tallies = tallies.at[1:1 + 2 * twos:2].set(donor - shifted).at[2:2 + 2 * twos:2].set(receiver + shifted)
    return tallies[jax.random.permutation(jax.random.fold_in(rng, 2), number_of)]


def gaussian(stream_key, extent, deviation, bound, cuts=(), kind=jnp.bfloat16):
    values = jax.random.normal(stream_key, extent, jnp.float32) * deviation
    if len(cuts) > 0:
        values = shard_levels(stream_key, extent, cuts, -0.22, 0.18) * values
    return jnp.clip(values, min=-bound, max=bound).astype(kind)


def setup_inputs(seed: int = 0) -> dict:
    key_of = jax.random.split(jax.random.key(seed), 17)
    return {
        "patches": draw_patches(jax.random.fold_in(key_of[16], 71), 0),
        "vis_gain": jnp.clip(1.0 + 0.15 * jax.random.normal(key_of[1], (D,), jnp.float32), 0.25, 1.75).astype(jnp.bfloat16),
        "vis_bias": gaussian(key_of[2], (D,), 0.5, 3.0, ((0, 8),)),
        "vis_qkv": draw_vis_qkv(jax.random.fold_in(key_of[16], 71), 0),
        "vis_qkv_bias": gaussian(key_of[4], (3 * D,), 0.5, 3.0, ((0, 16),)),
        "vis_out": gaussian(key_of[5], (D, D), D ** -0.5, 0.15625, ((0, 16), (1, 8))),
        "vis_out_bias": gaussian(key_of[6], (D,), 0.5, 3.0, ((0, 8),)),
        "proj_weight": gaussian(key_of[7], (4, D, D), (4 * D) ** -0.5, 0.078125, ((1, 8), (2, 16))),
        "proj_bias": gaussian(key_of[8], (D,), 0.5, 3.0, ((0, 16),)),
        "text_embeds": draw_text_embeds(jax.random.fold_in(key_of[16], 71), 0),
        "dec_gain": jnp.clip(1.0 + 0.15 * jax.random.normal(key_of[10], (D,), jnp.float32), 0.25, 1.75).astype(jnp.bfloat16),
        "dec_qkv": draw_dec_qkv(jax.random.fold_in(key_of[16], 71), 0),
        "dec_out": gaussian(key_of[12], (D, D), D ** -0.5, 0.15625, ((0, 8), (1, 16))),
        "image_tokens": jax.vmap(lambda own: ragged_sizes(own, IMGS, MH, MH // 4, 2))(jax.random.split(key_of[13], HALVES)).reshape((HALVES, IMGS)).astype(jnp.int32),
        "text_gaps": jax.vmap(lambda own: ragged_sizes(own, IMGS + 1, SH - MH, (SH - MH) // 2, 2))(jax.random.split(key_of[14], HALVES)).reshape((HALVES, IMGS + 1)).astype(jnp.int32),
        "doc_lengths": ragged_sizes(key_of[15], SEGS, 2 * SH, SH, 1).astype(jnp.int32),
    }


def segment_of(index_values, lengths):
    ends = jnp.cumsum(lengths, dtype=jnp.int32)
    return lax.optimization_barrier(jnp.sum((index_values[:, None] >= ends[None, :]).astype(jnp.int32), axis=1, dtype=jnp.int32))

def insert_map(text_rows, image_lengths, gaps):
    offsets = jnp.cumsum(image_lengths, dtype=jnp.int32) - image_lengths
    starts = jnp.cumsum(gaps, dtype=jnp.int32)[:image_lengths.shape[0]] + offsets
    inside = (text_rows[:, None] >= starts[None, :]) & (text_rows[:, None] < (starts + image_lengths)[None, :])
    source = lax.optimization_barrier(jnp.sum(jnp.where(inside, offsets[None, :] + text_rows[:, None] - starts[None, :], 0), axis=1, dtype=jnp.int32))
    return (source.astype(jnp.int32), jnp.any(inside, axis=1))

def attend_heads(query, keys, values, allowed, scale):

    def one_head(parts):
        head_q, head_k, head_v = parts
        scores = jnp.dot(head_q, head_k.T, preferred_element_type=jnp.float32) * scale
        scores = jnp.where(allowed, scores, -1e+30)
        top = lax.optimization_barrier(jnp.max(scores, axis=1, keepdims=True))
        weights = jnp.where(allowed, jnp.exp(scores - top), 0.0)
        total = lax.optimization_barrier(jnp.sum(weights, axis=1, keepdims=True))
        mixed = jnp.dot(weights.astype(jnp.bfloat16), head_v, preferred_element_type=jnp.float32) / total
        return mixed.astype(jnp.bfloat16)
    return lax.map(one_head, (query, keys, values))

def split_heads(rows, count):
    shaped = rows.reshape(count, HEADS, 3, HEAD_DIM)
    return (jnp.transpose(shaped[:, :, 0], (1, 0, 2)), jnp.transpose(shaped[:, :, 1], (1, 0, 2)), jnp.transpose(shaped[:, :, 2], (1, 0, 2)))

def reference(patches, vis_gain, vis_bias, vis_qkv, vis_qkv_bias, vis_out, vis_out_bias, proj_weight, proj_bias, text_embeds, dec_gain, dec_qkv, dec_out, image_tokens, text_gaps, doc_lengths):
    width = HEADS * HEAD_DIM
    scale = HEAD_DIM ** (-0.5)
    pieces = []
    for half in range(HALVES):
        xfull = patches[half].astype(jnp.float32)
        mean = lax.optimization_barrier(jnp.sum(xfull, axis=1, keepdims=True)) / width
        variance = lax.optimization_barrier(jnp.sum(xfull * xfull, axis=1, keepdims=True)) / width - mean * mean
        normed = ((xfull - mean) * lax.rsqrt(variance + 1e-06) * vis_gain.astype(jnp.float32) + vis_bias.astype(jnp.float32)).astype(jnp.bfloat16)
        qkv_rows = (jnp.dot(normed, vis_qkv, preferred_element_type=jnp.float32) + vis_qkv_bias.astype(jnp.float32)).astype(jnp.bfloat16)
        query, keys, values = split_heads(qkv_rows, PH)
        image_id = segment_of(jnp.arange(PH, dtype=jnp.int32) // 4, image_tokens[half])
        allowed = image_id[:, None] == image_id[None, :]
        heads_out = attend_heads(query, keys, values, allowed, scale)
        attn = jnp.transpose(heads_out, (1, 0, 2)).reshape(PH, width)
        resid = (xfull + jnp.dot(attn, vis_out, preferred_element_type=jnp.float32) + vis_out_bias.astype(jnp.float32)).astype(jnp.bfloat16)
        merged = resid.reshape(MH, 4 * width)
        projected = jnp.dot(merged, proj_weight.reshape(4 * width, width), preferred_element_type=jnp.float32)
        source, is_image = insert_map(jnp.arange(SH, dtype=jnp.int32), image_tokens[half], text_gaps[half])
        placed = jnp.take(projected, source, axis=0) + proj_bias.astype(jnp.float32)
        pieces.append(jnp.where(is_image[:, None], placed, text_embeds[half].astype(jnp.float32)).astype(jnp.bfloat16))
    stacked = jnp.stack(pieces, axis=0)
    total_rows = HALVES * SH
    dec_input = jnp.transpose(stacked.reshape(HALVES, SH // TPD, TPD, width), (1, 0, 2, 3)).reshape(total_rows, width)
    xf = dec_input.astype(jnp.float32)
    mean_square = lax.optimization_barrier(jnp.sum(xf * xf, axis=1, keepdims=True)) / width
    normed = (xf * lax.rsqrt(mean_square + 1e-05) * dec_gain.astype(jnp.float32)).astype(jnp.bfloat16)
    qkv_rows = jnp.dot(normed, dec_qkv, preferred_element_type=jnp.float32).astype(jnp.bfloat16)
    query, keys, values = split_heads(qkv_rows, total_rows)
    positions = jnp.arange(total_rows, dtype=jnp.int32)
    doc = segment_of(positions, doc_lengths)
    allowed = (doc[:, None] == doc[None, :]) & (positions[None, :] <= positions[:, None])
    heads_out = attend_heads(query, keys, values, allowed, scale)
    attn = jnp.transpose(heads_out, (1, 0, 2)).reshape(total_rows, width)
    hidden = (xf + jnp.dot(attn, dec_out, preferred_element_type=jnp.float32)).astype(jnp.bfloat16)
    return jnp.transpose(hidden.reshape(SH // TPD, HALVES, TPD, width), (1, 0, 2, 3)).reshape(HALVES, SH, width)
```

```python
import functools

import jax
import jax.numpy as jnp
from jax import lax
from jax.experimental import pallas as pl
from jax.experimental.pallas import tpu as pltpu
from jax.sharding import PartitionSpec as P

HEADS = 16
HEAD_DIM = 88
WIDTH = HEADS * HEAD_DIM
TPD = 256
LOG2E = 1.4426950408889634
NEG = -1e30
F32 = jnp.float32
BF16 = jnp.bfloat16


def spread(values, axes):
    count = lax.axis_size(axes)
    return lax.all_to_all(
        jnp.broadcast_to(values[None], (count,) + values.shape), axes, split_axis=0, concat_axis=0
    )


def exchange(values, axes):
    return lax.all_to_all(values, axes, split_axis=0, concat_axis=0)


def dot0(left, right):
    return lax.dot_general(left, right, (((0,), (0,)), ((), ())), preferred_element_type=F32)


def segment_of(index_values, lengths):
    ends = jnp.cumsum(lengths, dtype=jnp.int32)
    return jnp.sum(
        (index_values[:, None] >= ends[None, :]).astype(jnp.int32), axis=1, dtype=jnp.int32
    )


def image_starts(lengths, gaps):
    offsets = jnp.cumsum(lengths, dtype=jnp.int32) - lengths
    return jnp.cumsum(gaps, dtype=jnp.int32)[: lengths.shape[0]] + offsets, offsets


def insert_map(text_rows, lengths, gaps):
    starts, offsets = image_starts(lengths, gaps)
    inside = (text_rows[:, None] >= starts[None, :]) & (
        text_rows[:, None] < (starts + lengths)[None, :]
    )
    source = jnp.sum(
        jnp.where(inside, offsets[None, :] + text_rows[:, None] - starts[None, :], 0),
        axis=1,
        dtype=jnp.int32,
    )
    return source, jnp.any(inside, axis=1)


def rows_of_merged(merged, lengths, gaps):
    starts, offsets = image_starts(lengths, gaps)
    inside = (merged[:, None] >= offsets[None, :]) & (
        merged[:, None] < (offsets + lengths)[None, :]
    )
    return jnp.sum(
        jnp.where(inside, starts[None, :] + merged[:, None] - offsets[None, :], 0),
        axis=1,
        dtype=jnp.int32,
    )


def sequence_position(rows, half):
    return (rows // TPD) * (2 * TPD) + half * TPD + rows % TPD


def decoder_kernel(
    bounds_ref, q_ref, kv_ref, bias_ref, image_kv_ref, image_pos_ref, qpos_ref, out_ref, acc_ref
):
    rows = q_ref.shape[1]
    block = kv_ref.shape[4]
    factor = LOG2E * HEAD_DIM ** (-0.5)
    query = q_ref[...]
    low = qpos_ref[0:1, :]
    span = qpos_ref[1:2, :]
    acc_ref[...] = jnp.zeros_like(acc_ref)

    def fold(state, keys, values, key_pos):
        best, total = state
        scores = dot0(keys, query)
        offset = key_pos - low
        allowed = (offset >= 0) & (offset <= span)
        scores = jnp.where(allowed, scores, NEG)
        new_best = jnp.maximum(best, jnp.max(scores, axis=0, keepdims=True))
        weights = jnp.exp2((scores - new_best) * factor)
        keep = jnp.exp2((best - new_best) * factor)
        total = total * keep + jnp.sum(weights, axis=0, keepdims=True)
        acc_ref[...] = acc_ref[...] * keep + jnp.dot(
            values, weights.astype(BF16), preferred_element_type=F32
        )
        return new_best, total

    state = (jnp.full((1, rows), NEG, F32), jnp.zeros((1, rows), F32))
    image_keys = jnp.concatenate(
        [image_kv_ref[0], jnp.zeros((8, image_kv_ref.shape[2]), BF16)], axis=0
    )
    state = fold(state, image_keys, image_kv_ref[1], image_pos_ref[...])
    step = lax.broadcasted_iota(jnp.int32, (block, 1), 0)
    in_pair = jnp.where(step >= TPD, step + TPD, step)

    def chunk(index, state):
        for half in range(2):
            keys = jnp.concatenate([kv_ref[index, half, 0], bias_ref[index, half]], axis=0)
            base = index * (2 * block) + half * TPD
            state = fold(state, keys, kv_ref[index, half, 1], in_pair + base)
        return state

    best, total = lax.fori_loop(bounds_ref[0], bounds_ref[1], chunk, state)
    out_ref[...] = (acc_ref[...] / total).astype(BF16)


def decoder_attention(bounds, query, keyval, bias, image_keyval, image_pos, qpos):
    vmem = pl.BlockSpec(memory_space=pltpu.VMEM)
    return pl.pallas_call(
        decoder_kernel,
        out_shape=jax.ShapeDtypeStruct((HEAD_DIM, query.shape[1]), BF16),
        in_specs=[pl.BlockSpec(memory_space=pltpu.SMEM)] + [vmem] * 6,
        out_specs=vmem,
        scratch_shapes=[pltpu.VMEM((HEAD_DIM, query.shape[1]), F32)],
        compiler_params=pltpu.CompilerParams(vmem_limit_bytes=32 * 1024 * 1024),
        name="decoder_attention",
    )(bounds, query, keyval, bias, image_keyval, image_pos, qpos)


def per_device(
    patches,
    vis_gain,
    vis_bias,
    vis_qkv,
    vis_qkv_bias,
    vis_out,
    vis_out_bias,
    proj_weight,
    proj_bias,
    text_embeds,
    dec_gain,
    dec_qkv,
    dec_out,
    image_tokens,
    text_gaps,
    doc_lengths,
):
    cols = lax.axis_size("col")
    rows = lax.axis_size("row")
    row = lax.axis_index("row")
    col = lax.axis_index("col")
    half = lax.axis_index("grp")
    scale = HEAD_DIM ** (-0.5)
    lengths, gaps = image_tokens[0], text_gaps[0]
    images = lengths.shape[0]

    table = jnp.concatenate([lengths, gaps])
    other_table = lax.ppermute(table, "grp", [(0, 1), (1, 0)])
    tables = jnp.where(
        half == 0, jnp.stack([table, other_table]), jnp.stack([other_table, table])
    )
    both_lengths, both_gaps = tables[:, :images], tables[:, images:]

    feat_c = vis_out.shape[1]
    packed = jnp.concatenate(
        [
            dec_qkv,
            vis_out,
            jnp.transpose(proj_weight, (2, 0, 1)).reshape(HEAD_DIM, 4 * feat_c),
            dec_out.T,
        ],
        axis=1,
    )
    gathered_w = lax.all_gather(packed, "col", axis=0)
    qkv_w = dec_qkv.shape[1]

    rows_b = patches.shape[1]
    part = rows_b // cols
    mine = exchange(patches[0].reshape(cols, part, feat_c), "col")
    mine = jnp.transpose(mine, (1, 0, 2)).reshape(part, WIDTH)
    raw = spread(mine, "row").reshape(rows * part, WIDTH)
    vis_w = spread(
        jnp.concatenate(
            [vis_qkv, vis_gain[:, None], vis_bias[:, None], vis_out_bias[:, None]], axis=1
        ),
        "col",
    ).reshape(WIDTH, -1)
    vis_n = vis_qkv.shape[1]
    affine = vis_w[:, vis_n:].T.astype(F32)
    xfull = raw.astype(F32)
    mean = jnp.sum(xfull, axis=1, keepdims=True) / WIDTH
    variance = jnp.sum(xfull * xfull, axis=1, keepdims=True) / WIDTH - mean * mean
    normed = (
        (xfull - mean) * lax.rsqrt(variance + 1e-06) * affine[0:1] + affine[1:2]
    ).astype(BF16)
    qkv_rows = (
        jnp.dot(normed, vis_w[:, :vis_n], preferred_element_type=F32) + vis_qkv_bias.astype(F32)
    ).astype(BF16)

    text = text_embeds[0].T
    positions = text.shape[1]
    text, gathered_w = lax.optimization_barrier((text, gathered_w))
    text_all = lax.all_gather(text, "row", axis=0, tiled=True)

    heads_w = jnp.transpose(
        gathered_w[:, :, :qkv_w].reshape(cols, HEAD_DIM, 2, 3 * HEAD_DIM), (0, 2, 1, 3)
    ).reshape(rows, HEAD_DIM, 3 * HEAD_DIM)
    outs_w = jnp.transpose(
        gathered_w[:, :, qkv_w : qkv_w + feat_c].reshape(cols, HEAD_DIM, 2, HEAD_DIM), (0, 2, 1, 3)
    ).reshape(rows, HEAD_DIM, HEAD_DIM)
    gain = jnp.broadcast_to(dec_gain[None, :, None], (rows, HEAD_DIM, 1))
    row_w = exchange(jnp.concatenate([heads_w, outs_w, gain], axis=2), "row").reshape(WIDTH, -1)
    head_w = row_w[:, : 3 * HEAD_DIM]
    out_w = row_w[:, 3 * HEAD_DIM : 4 * HEAD_DIM]
    gain_all = row_w[:, 4 * HEAD_DIM :].astype(F32)
    proj_at = qkv_w + feat_c
    proj_w = jnp.transpose(
        gathered_w[:, :, proj_at : proj_at + 4 * feat_c].reshape(cols, HEAD_DIM, 4, feat_c),
        (2, 1, 0, 3),
    ).reshape(4, HEAD_DIM, WIDTH)
    dec_out_w = jnp.transpose(gathered_w[:, :, proj_at + 4 * feat_c :], (1, 0, 2)).reshape(
        HEAD_DIM, WIDTH
    )

    xtext = text_all.astype(F32)
    squares = jnp.sum(xtext * xtext, axis=0, keepdims=True)
    text_normed = (xtext * lax.rsqrt(squares / WIDTH + 1e-05) * gain_all).astype(BF16)
    text_qkv = dot0(head_w, text_normed).astype(BF16)
    own_kv = text_qkv[HEAD_DIM:]
    other_kv = lax.ppermute(own_kv, "grp", [(0, 1), (1, 0)])
    pair_kv = jnp.where(half == 0, jnp.stack([own_kv, other_kv]), jnp.stack([other_kv, own_kv]))
    all_kv = lax.all_gather(pair_kv, "col", axis=0).reshape(cols, 2, 2, HEAD_DIM, positions)

    count = rows * part
    query = qkv_rows[:, :HEAD_DIM]
    keyval = spread(qkv_rows[:, HEAD_DIM:], "col").reshape(cols * count, 2 * HEAD_DIM)
    keys, values = keyval[:, :HEAD_DIM], keyval[:, HEAD_DIM:]

    def patch_index(col_index, inner):
        return (inner // part) * rows_b + col_index * part + inner % part

    inner = jnp.arange(count, dtype=jnp.int32)
    query_ids = segment_of(patch_index(col, inner) // 4, lengths)
    every = jnp.arange(cols * count, dtype=jnp.int32)
    key_ids = segment_of(patch_index(every // count, every % count) // 4, lengths)
    allowed = query_ids[:, None] == key_ids[None, :]
    scores = (
        lax.dot_general(query, keys, (((1,), (1,)), ((), ())), preferred_element_type=F32) * scale
    )
    scores = jnp.where(allowed, scores, NEG)
    weights = jnp.where(allowed, jnp.exp(scores - jnp.max(scores, axis=1, keepdims=True)), 0.0)
    total = jnp.sum(weights, axis=1, keepdims=True)
    vis_attn = (jnp.dot(weights.astype(BF16), values, preferred_element_type=F32) / total).astype(
        BF16
    )

    def window_first(array):
        features = array.shape[1]
        return jnp.transpose(
            array.reshape(rows, part // 4, 4, features), (2, 0, 1, 3)
        ).reshape(count, features)

    own_raw = window_first(lax.dynamic_slice(raw, (0, row * HEAD_DIM), (count, HEAD_DIM)))
    own_bias = lax.dynamic_slice(affine[2], (row * HEAD_DIM,), (HEAD_DIM,))
    all_attn = spread(window_first(vis_attn).T, "row").reshape(WIDTH, count)
    resid = (own_raw.T.astype(F32) + dot0(out_w, all_attn) + own_bias[:, None]).astype(BF16)
    all_resid = spread(resid, "row").reshape(WIDTH, count)
    merged = count // 4
    projected = proj_bias.astype(F32)[:, None]
    for window in range(4):
        projected = projected + jnp.dot(
            proj_w[window],
            all_resid[:, window * merged : (window + 1) * merged],
            preferred_element_type=F32,
        )
    image_in = projected.T.astype(BF16)

    image_all = jnp.transpose(spread(image_in, "row"), (1, 0, 2)).reshape(merged, WIDTH)
    ximage = image_all.astype(F32)
    squares = jnp.sum(ximage * ximage, axis=1, keepdims=True)
    image_normed = (
        ximage * lax.rsqrt(squares / WIDTH + 1e-05) * gain_all[:, 0][None, :]
    ).astype(BF16)
    image_qkv = jnp.dot(image_normed, head_w, preferred_element_type=F32).astype(BF16)
    shared = spread(jnp.concatenate([image_qkv, image_in], axis=1), ("col", "grp"))
    shared = shared.reshape(cols, 2, merged, 4 * HEAD_DIM)

    own_rows = col * positions + jnp.arange(positions, dtype=jnp.int32)
    source, inside = insert_map(own_rows, lengths, gaps)
    pair = part // 4
    slot = (source // pair % cols) * merged + source // (pair * cols) * pair + source % pair
    chosen = (
        (slot[None, :] == jnp.arange(cols * merged, dtype=jnp.int32)[:, None]) & inside[None, :]
    ).astype(BF16)
    own_half = lax.dynamic_index_in_dim(shared, half, axis=1, keepdims=False)
    own_half = own_half.reshape(cols * merged, 4 * HEAD_DIM)
    placed_q = dot0(own_half[:, :HEAD_DIM], chosen).astype(BF16)
    placed_in = dot0(own_half[:, 3 * HEAD_DIM :], chosen)
    own_query = jnp.where(inside[None, :], placed_q, text_qkv[:HEAD_DIM])
    dec_input = jnp.where(inside[None, :], placed_in, text.astype(F32))
    query_aug = jnp.concatenate(
        [own_query, jnp.ones((1, positions), BF16), jnp.zeros((7, positions), BF16)], axis=0
    )
    all_rows = jnp.arange(cols * positions, dtype=jnp.int32)
    masks = [insert_map(all_rows, both_lengths[h], both_gaps[h])[1] for h in range(2)]
    bias = jnp.where(jnp.stack(masks), NEG, 0.0).astype(BF16).reshape(2, cols, 1, positions)
    bias = jnp.pad(jnp.transpose(bias, (1, 0, 2, 3)), ((0, 0), (0, 0), (0, 7), (0, 0)))
    item = jnp.arange(cols * merged, dtype=jnp.int32)
    merged_id = (item % merged) // pair * (pair * cols) + (item // merged) * pair + item % pair
    image_pos = jnp.stack(
        [
            sequence_position(rows_of_merged(merged_id, both_lengths[h], both_gaps[h]), h)
            for h in range(2)
        ]
    )
    image_pos = jnp.transpose(image_pos.reshape(2, cols, merged), (1, 0, 2)).reshape(-1, 1)
    image_kv = jnp.transpose(
        shared[..., HEAD_DIM : 3 * HEAD_DIM].reshape(cols * 2 * merged, 2, HEAD_DIM), (1, 2, 0)
    )
    query_pos = sequence_position(own_rows, half)
    ends = jnp.cumsum(doc_lengths, dtype=jnp.int32)
    low = jnp.max(
        jnp.where(query_pos[:, None] >= ends[None, :], ends[None, :], 0), axis=1
    )
    qpos = jnp.stack([low, query_pos - low])
    bounds = jnp.stack([jnp.min(low) // (2 * positions), col + 1]).astype(jnp.int32)
    dec_attn = decoder_attention(bounds, query_aug, all_kv, bias, image_kv, image_pos, qpos)

    all_dec = spread(dec_attn, "row").reshape(WIDTH, positions)
    delta = jnp.dot(dec_out_w, all_dec, preferred_element_type=F32)
    return (dec_input + delta).astype(BF16).T[None]


def solution(mesh):
    return jax.shard_map(
        per_device,
        mesh=mesh,
        in_specs=(
            P("grp", "row", "col"),
            P("col"),
            P("col"),
            P("col", "row"),
            P("row"),
            P("row", "col"),
            P("col"),
            P(None, "col", "row"),
            P("row"),
            P("grp", "col", "row"),
            P("row"),
            P("row", "col"),
            P("col", "row"),
            P("grp", None),
            P("grp", None),
            P(),
        ),
        out_specs=P("grp", "col", "row"),
        check_vma=False,
    )
```

```python
import functools

import jax
import jax.numpy as jnp
from jax import lax
from jax.experimental import pallas as pl
from jax.experimental.pallas import tpu as pltpu
from jax.sharding import PartitionSpec as P

HEADS = 16
HEAD_DIM = 88
WIDTH = HEADS * HEAD_DIM
TPD = 256
LOG2E = 1.4426950408889634
NEG = -1e30
F32 = jnp.float32
BF16 = jnp.bfloat16


def spread(values, axes):
    count = lax.axis_size(axes)
    return lax.all_to_all(
        jnp.broadcast_to(values[None], (count,) + values.shape), axes, split_axis=0, concat_axis=0
    )


def exchange(values, axes):
    return lax.all_to_all(values, axes, split_axis=0, concat_axis=0)


def dot0(left, right):
    return lax.dot_general(left, right, (((0,), (0,)), ((), ())), preferred_element_type=F32)


def running(lengths):
    at = jnp.arange(lengths.shape[0], dtype=jnp.int32)
    return jnp.sum(
        jnp.where(at[None, :] <= at[:, None], lengths[None, :], 0), axis=1, dtype=jnp.int32
    )


def segment_of(index_values, lengths):
    ends = running(lengths)
    return jnp.sum(
        (index_values[:, None] >= ends[None, :]).astype(jnp.int32), axis=1, dtype=jnp.int32
    )


def image_starts(lengths, gaps):
    offsets = running(lengths) - lengths
    return running(gaps)[: lengths.shape[0]] + offsets, offsets


def insert_map(text_rows, lengths, gaps):
    starts, offsets = image_starts(lengths, gaps)
    inside = (text_rows[:, None] >= starts[None, :]) & (
        text_rows[:, None] < (starts + lengths)[None, :]
    )
    source = jnp.sum(
        jnp.where(inside, offsets[None, :] + text_rows[:, None] - starts[None, :], 0),
        axis=1,
        dtype=jnp.int32,
    )
    return source, jnp.any(inside, axis=1)


def rows_of_merged(merged, lengths, gaps):
    starts, offsets = image_starts(lengths, gaps)
    inside = (merged[:, None] >= offsets[None, :]) & (
        merged[:, None] < (offsets + lengths)[None, :]
    )
    return jnp.sum(
        jnp.where(inside, starts[None, :] + merged[:, None] - offsets[None, :], 0),
        axis=1,
        dtype=jnp.int32,
    )


def sequence_position(rows, half):
    return (rows // TPD) * (2 * TPD) + half * TPD + rows % TPD


def decoder_kernel(
    bounds_ref, q_ref, kv_ref, image_kv_ref, image_pos_ref, qpos_ref, out_ref, acc_ref
):
    rows = q_ref.shape[1]
    block = kv_ref.shape[3]
    key_rows = q_ref.shape[0]
    factor = LOG2E * HEAD_DIM ** (-0.5)
    query = q_ref[...]
    low = qpos_ref[0:1, :]
    span = qpos_ref[1:2, :]
    acc_ref[...] = jnp.zeros_like(acc_ref)

    def fold(state, keys, values, key_pos):
        best, total = state
        scores = dot0(keys, query)
        offset = key_pos - low
        allowed = (offset >= 0) & (offset <= span)
        scores = jnp.where(allowed, scores, NEG)
        new_best = jnp.maximum(best, jnp.max(scores, axis=0, keepdims=True))
        weights = jnp.exp2((scores - new_best) * factor)
        keep = jnp.exp2((best - new_best) * factor)
        total = total * keep + jnp.sum(weights, axis=0, keepdims=True)
        acc_ref[...] = acc_ref[...] * keep + jnp.dot(
            values, weights.astype(BF16), preferred_element_type=F32
        )
        return new_best, total

    state = (jnp.full((1, rows), NEG, F32), jnp.zeros((1, rows), F32))
    state = fold(state, image_kv_ref[:key_rows], image_kv_ref[key_rows:], image_pos_ref[...])
    step = lax.broadcasted_iota(jnp.int32, (block, 1), 0)
    in_pair = jnp.where(step >= TPD, step + TPD, step)

    def chunk(index, state):
        for half in range(2):
            keys = kv_ref[index, half, :key_rows]
            values = kv_ref[index, half, key_rows:]
            base = index * (2 * block) + half * TPD
            state = fold(state, keys, values, in_pair + base)
        return state

    best, total = lax.fori_loop(bounds_ref[0], bounds_ref[1], chunk, state)
    out_ref[...] = (acc_ref[...] / total).astype(BF16)


def decoder_attention(bounds, query, keyval, image_keyval, image_pos, qpos):
    vmem = pl.BlockSpec(memory_space=pltpu.VMEM)
    return pl.pallas_call(
        decoder_kernel,
        out_shape=jax.ShapeDtypeStruct((HEAD_DIM, query.shape[1]), BF16),
        in_specs=[pl.BlockSpec(memory_space=pltpu.SMEM)] + [vmem] * 5,
        out_specs=vmem,
        scratch_shapes=[pltpu.VMEM((HEAD_DIM, query.shape[1]), F32)],
        compiler_params=pltpu.CompilerParams(vmem_limit_bytes=32 * 1024 * 1024),
        name="decoder_attention",
    )(bounds, query, keyval, image_keyval, image_pos, qpos)


def per_device(
    patches,
    vis_gain,
    vis_bias,
    vis_qkv,
    vis_qkv_bias,
    vis_out,
    vis_out_bias,
    proj_weight,
    proj_bias,
    text_embeds,
    dec_gain,
    dec_qkv,
    dec_out,
    image_tokens,
    text_gaps,
    doc_lengths,
):
    cols = lax.axis_size("col")
    rows = lax.axis_size("row")
    row = lax.axis_index("row")
    col = lax.axis_index("col")
    half = lax.axis_index("grp")
    scale = HEAD_DIM ** (-0.5)

    feat_c = vis_out.shape[1]
    vis_n = vis_qkv.shape[1]
    unit = -(-(vis_n + HEAD_DIM) // 128) * 128
    fill = jnp.zeros((HEAD_DIM, unit - vis_n - HEAD_DIM), BF16)
    sides = (slice(0, HEAD_DIM), slice(HEAD_DIM, 2 * HEAD_DIM))
    units = [
        [dec_qkv[:, at * vis_n : (at + 1) * vis_n], vis_out[:, side], fill]
        for at, side in enumerate(sides)
    ]
    units += [[vis_qkv[side], dec_out[side], fill] for side in sides]
    units += [[proj_weight[window, side] for window in range(4)] + [fill] for side in sides]
    packed = jnp.stack([jnp.concatenate(pieces, axis=1) for pieces in units])
    gathered_w = lax.all_gather(packed, "col", axis=0)

    def pair(number):
        return gathered_w[:, 2 * number : 2 * number + 2]

    rows_b = patches.shape[1]
    part = rows_b // cols
    affine_own = jnp.stack([vis_gain, vis_bias, vis_out_bias])
    affine_own = jnp.pad(affine_own, ((0, 8 - affine_own.shape[0]), (0, 0)))
    mine = exchange(
        jnp.concatenate(
            [
                patches[0].reshape(cols, part, feat_c),
                jnp.broadcast_to(affine_own[None], (cols, 8, feat_c)),
            ],
            axis=1,
        ),
        "col",
    )
    mine = jnp.transpose(mine, (1, 0, 2)).reshape(part + 8, WIDTH)
    affine = mine[part : part + 3].astype(F32)

    text = text_embeds[0].T
    positions = text.shape[1]
    folds = -(-(WIDTH + HEAD_DIM) // positions)
    spare = folds * positions - WIDTH
    gain = jnp.broadcast_to(jnp.pad(dec_gain, (0, spare - HEAD_DIM))[None], (part, spare))
    folded = jnp.concatenate([mine[:part], gain], axis=1)
    folded = jnp.transpose(folded.reshape(part, folds, positions), (1, 0, 2))
    both = spread(
        jnp.concatenate([text, folded.reshape(folds * part, positions)], axis=0), "row"
    )
    text_all = both[:, :HEAD_DIM].reshape(WIDTH, positions)
    raw = jnp.transpose(
        both[:, HEAD_DIM:].reshape(rows, folds, part, positions), (0, 2, 1, 3)
    ).reshape(rows, part, folds * positions)
    gain_all = raw[:, 0, WIDTH : WIDTH + HEAD_DIM].reshape(WIDTH, 1).astype(F32)
    raw = raw[:, :, :WIDTH].reshape(rows * part, WIDTH)
    xtext = text_all.astype(F32)
    squares = jnp.sum(xtext * xtext, axis=0, keepdims=True)
    text_normed = (xtext * lax.rsqrt(squares / WIDTH + 1e-05) * gain_all).astype(BF16)

    row_w = exchange(pair(0).reshape(rows, HEAD_DIM, unit), "row").reshape(WIDTH, unit)

    vis_w = pair(1).reshape(WIDTH, unit)
    xfull = raw.astype(F32)
    mean = jnp.sum(xfull, axis=1, keepdims=True) / WIDTH
    variance = jnp.sum(xfull * xfull, axis=1, keepdims=True) / WIDTH - mean * mean
    normed = (
        (xfull - mean) * lax.rsqrt(variance + 1e-06) * affine[0:1] + affine[1:2]
    ).astype(BF16)
    qkv_rows = (
        jnp.dot(normed, vis_w, preferred_element_type=F32)[:, :vis_n]
        + vis_qkv_bias.astype(F32)
    ).astype(BF16)
    count = rows * part
    query = qkv_rows[:, :HEAD_DIM]
    row_w, vis_kv = lax.optimization_barrier((row_w, qkv_rows[:, HEAD_DIM:]))
    lengths, gaps = image_tokens[0], text_gaps[0]
    own_rows = col * positions + jnp.arange(positions, dtype=jnp.int32)
    source, inside = insert_map(own_rows, lengths, gaps)
    keyval = spread(vis_kv, "col").reshape(cols * count, 2 * HEAD_DIM)
    proj_w = pair(2).reshape(WIDTH, unit)
    dec_out_w = vis_w[:, vis_n : vis_n + HEAD_DIM]

    text_qkv = dot0(row_w, text_normed)[:vis_n].astype(BF16)
    bias = jnp.where(inside, NEG, 0.0).astype(BF16)[None]
    own_kv = jnp.concatenate(
        [
            text_qkv[HEAD_DIM : 2 * HEAD_DIM],
            jnp.pad(bias, ((0, 7), (0, 0))),
            text_qkv[2 * HEAD_DIM :],
        ],
        axis=0,
    )
    other_kv = lax.ppermute(own_kv, "grp", [(0, 1), (1, 0)])
    pair_kv = jnp.where(half == 0, jnp.stack([own_kv, other_kv]), jnp.stack([other_kv, own_kv]))
    pair_kv, keyval = lax.optimization_barrier((pair_kv, keyval))
    all_kv = lax.all_gather(pair_kv, "col", axis=0)

    keys, values = keyval[:, :HEAD_DIM], keyval[:, HEAD_DIM:]

    def patch_index(col_index, inner):
        return (inner // part) * rows_b + col_index * part + inner % part

    inner = jnp.arange(count, dtype=jnp.int32)
    query_ids = segment_of(patch_index(col, inner) // 4, lengths)
    every = jnp.arange(cols * count, dtype=jnp.int32)
    key_ids = segment_of(patch_index(every // count, every % count) // 4, lengths)
    allowed = query_ids[:, None] == key_ids[None, :]
    scores = (
        lax.dot_general(query, keys, (((1,), (1,)), ((), ())), preferred_element_type=F32) * scale
    )
    scores = jnp.where(allowed, scores, NEG)
    weights = jnp.where(allowed, jnp.exp(scores - jnp.max(scores, axis=1, keepdims=True)), 0.0)
    total = jnp.sum(weights, axis=1, keepdims=True)
    vis_attn = (jnp.dot(weights.astype(BF16), values, preferred_element_type=F32) / total).astype(
        BF16
    )

    def window_first(array):
        features = array.shape[1]
        return jnp.transpose(
            array.reshape(rows, part // 4, 4, features), (2, 0, 1, 3)
        ).reshape(count, features)

    raw_at = row * HEAD_DIM
    own_raw = window_first(lax.dynamic_slice(raw, (0, raw_at), (count, HEAD_DIM)))
    own_bias = lax.dynamic_slice(affine[2], (raw_at,), (HEAD_DIM,))
    all_attn = spread(window_first(vis_attn).T, "row").reshape(WIDTH, count)
    resid = (own_raw.T.astype(F32) + dot0(row_w, all_attn)[vis_n : vis_n + HEAD_DIM] + own_bias[:, None]).astype(BF16)
    all_resid = spread(resid, "row").reshape(WIDTH, count)
    merged = count // 4
    windows = dot0(proj_w, all_resid)
    projected = proj_bias.astype(F32)[:, None]
    for window in range(4):
        projected = projected + windows[
            window * HEAD_DIM : (window + 1) * HEAD_DIM, window * merged : (window + 1) * merged
        ]
    image_in = projected.T.astype(BF16)

    image_all = jnp.transpose(spread(image_in, "row"), (1, 0, 2)).reshape(merged, WIDTH)
    ximage = image_all.astype(F32)
    squares = jnp.sum(ximage * ximage, axis=1, keepdims=True)
    image_normed = (
        ximage * lax.rsqrt(squares / WIDTH + 1e-05) * gain_all[:, 0][None, :]
    ).astype(BF16)
    image_qkv = jnp.dot(image_normed, row_w, preferred_element_type=F32)[:, :vis_n].astype(BF16)
    pack = part // 4
    item = jnp.arange(merged, dtype=jnp.int32)
    merged_id = item // pack * (pack * cols) + col * pack + item % pack
    place = sequence_position(rows_of_merged(merged_id, lengths, gaps), half)
    place = jnp.stack([place // 64, place % 64], axis=1).astype(BF16)
    shared = spread(
        jnp.concatenate(
            [
                image_qkv[:, : 2 * HEAD_DIM],
                jnp.zeros((merged, 8), BF16),
                image_qkv[:, 2 * HEAD_DIM :],
                image_in,
                place,
            ],
            axis=1,
        ),
        ("col", "grp"),
    )
    key_at, in_at = HEAD_DIM, 3 * HEAD_DIM + 8
    place_at = in_at + HEAD_DIM
    everything = shared.reshape(cols * 2 * merged, -1)
    shared = shared.reshape(cols, 2, merged, -1)

    slot = (source // pack % cols) * merged + source // (pack * cols) * pack + source % pack
    chosen = (
        (slot[None, :] == jnp.arange(cols * merged, dtype=jnp.int32)[:, None]) & inside[None, :]
    ).astype(BF16)
    own_half = lax.dynamic_index_in_dim(shared, half, axis=1, keepdims=False)
    own_half = own_half.reshape(cols * merged, -1)
    placed = dot0(own_half, chosen)
    own_query = jnp.where(
        inside[None, :], placed[:HEAD_DIM].astype(BF16), text_qkv[:HEAD_DIM]
    )
    dec_input = jnp.where(inside[None, :], placed[in_at : in_at + HEAD_DIM], text.astype(F32))
    query_aug = jnp.concatenate(
        [own_query, jnp.ones((1, positions), BF16), jnp.zeros((7, positions), BF16)], axis=0
    )
    image_kv = everything[:, key_at:in_at].T
    place = everything[:, place_at : place_at + 2].astype(jnp.int32)
    image_pos = place[:, :1] * 64 + place[:, 1:]
    query_pos = sequence_position(own_rows, half)
    ends = running(doc_lengths)
    low = jnp.max(
        jnp.where(query_pos[:, None] >= ends[None, :], ends[None, :], 0), axis=1
    )
    qpos = jnp.stack([low, query_pos - low])
    bounds = jnp.stack([jnp.min(low) // (2 * positions), col + 1]).astype(jnp.int32)
    dec_attn = decoder_attention(bounds, query_aug, all_kv, image_kv, image_pos, qpos)

    all_dec = spread(dec_attn, "row").reshape(WIDTH, positions)
    delta = dot0(dec_out_w, all_dec)
    return (dec_input + delta).astype(BF16).T[None]


def solution(mesh):
    return jax.shard_map(
        per_device,
        mesh=mesh,
        in_specs=(
            P("grp", "row", "col"),
            P("col"),
            P("col"),
            P("col", "row"),
            P("row"),
            P("row", "col"),
            P("col"),
            P(None, "col", "row"),
            P("row"),
            P("grp", "col", "row"),
            P("row"),
            P("row", "col"),
            P("col", "row"),
            P("grp", None),
            P("grp", None),
            P(),
        ),
        out_specs=P("grp", "col", "row"),
        check_vma=False,
    )
```

```python
import functools

import jax
import jax.numpy as jnp
from jax import lax
from jax.experimental import pallas as pl
from jax.experimental.pallas import tpu as pltpu
from jax.sharding import PartitionSpec as P

HEADS = 16
HEAD_DIM = 88
WIDTH = HEADS * HEAD_DIM
TPD = 256
LOG2E = 1.4426950408889634
NEG = -1e30
F32 = jnp.float32
BF16 = jnp.bfloat16


def spread(values, axes):
    count = lax.axis_size(axes)
    return lax.all_to_all(
        jnp.broadcast_to(values[None], (count,) + values.shape), axes, split_axis=0, concat_axis=0
    )


def exchange(values, axes):
    return lax.all_to_all(values, axes, split_axis=0, concat_axis=0)


def dot0(left, right):
    return lax.dot_general(left, right, (((0,), (0,)), ((), ())), preferred_element_type=F32)


def running(lengths):
    at = jnp.arange(lengths.shape[0], dtype=jnp.int32)
    return jnp.sum(
        jnp.where(at[None, :] <= at[:, None], lengths[None, :], 0), axis=1, dtype=jnp.int32
    )


def segment_of(index_values, lengths):
    ends = running(lengths)
    return jnp.sum(
        (index_values[:, None] >= ends[None, :]).astype(jnp.int32), axis=1, dtype=jnp.int32
    )


def image_starts(lengths, gaps):
    offsets = running(lengths) - lengths
    return running(gaps)[: lengths.shape[0]] + offsets, offsets


def insert_map(text_rows, lengths, gaps):
    starts, offsets = image_starts(lengths, gaps)
    inside = (text_rows[:, None] >= starts[None, :]) & (
        text_rows[:, None] < (starts + lengths)[None, :]
    )
    source = jnp.sum(
        jnp.where(inside, offsets[None, :] + text_rows[:, None] - starts[None, :], 0),
        axis=1,
        dtype=jnp.int32,
    )
    return source, jnp.any(inside, axis=1)


def rows_of_merged(merged, lengths, gaps):
    starts, offsets = image_starts(lengths, gaps)
    inside = (merged[:, None] >= offsets[None, :]) & (
        merged[:, None] < (offsets + lengths)[None, :]
    )
    return jnp.sum(
        jnp.where(inside, starts[None, :] + merged[:, None] - offsets[None, :], 0),
        axis=1,
        dtype=jnp.int32,
    )


def sequence_position(rows, half):
    return (rows // TPD) * (2 * TPD) + half * TPD + rows % TPD


def fold_block(state, query, keys, values, key_pos, low, span, chosen=None):
    best, total, mixed = state
    factor = LOG2E * HEAD_DIM ** (-0.5)
    scores = dot0(keys, query)
    offset = key_pos - low
    allowed = (offset >= 0) & (offset <= span)
    if chosen is not None:
        allowed = allowed & chosen
    scores = jnp.where(allowed, scores, NEG)
    new_best = jnp.maximum(best, jnp.max(scores, axis=0, keepdims=True))
    weights = jnp.exp2((scores - new_best) * factor)
    keep = jnp.exp2((best - new_best) * factor)
    total = total * keep + jnp.sum(weights, axis=0, keepdims=True)
    added = jnp.dot(values, weights.astype(BF16), preferred_element_type=F32)
    return new_best, total, mixed * keep + added


def fold_text(bounds_ref, kv_ref, state, query, low, span, chosen=None):
    block = kv_ref.shape[3]
    key_rows = query.shape[0]
    step = lax.broadcasted_iota(jnp.int32, (block, 1), 0)
    in_pair = jnp.where(step >= TPD, step + TPD, step)

    def chunk(index, state):
        for half in range(2):
            keys = kv_ref[index, half, :key_rows]
            values = kv_ref[index, half, key_rows:]
            key_pos = in_pair + (index * (2 * block) + half * TPD)
            state = fold_block(state, query, keys, values, key_pos, low, span, chosen)
        return state

    return lax.fori_loop(bounds_ref[0], bounds_ref[1], chunk, state)


def text_kernel(bounds_ref, q_ref, kv_ref, qpos_ref, mix_ref, stat_ref):
    count = q_ref.shape[1]
    state = (
        jnp.full((1, count), NEG, F32),
        jnp.zeros((1, count), F32),
        jnp.zeros((HEAD_DIM, count), F32),
    )
    best, total, mixed = fold_text(
        bounds_ref, kv_ref, state, q_ref[...], qpos_ref[0:1, :], qpos_ref[1:2, :]
    )
    stat_ref[0:1, :] = best
    stat_ref[1:2, :] = total
    mix_ref[...] = mixed


KEY_AT = HEAD_DIM
VALUE_AT = 2 * HEAD_DIM + 8
INPUT_AT = VALUE_AT + HEAD_DIM
PLACE_AT = INPUT_AT + HEAD_DIM


def image_kernel(
    bounds_ref,
    busy_ref,
    shared_ref,
    text_ref,
    text_q_ref,
    kv_ref,
    qpos_ref,
    text_mix_ref,
    text_stat_ref,
    out_ref,
    input_ref,
    query_ref,
    mix_ref,
    stat_ref,
):
    shared = shared_ref[...]
    slot = qpos_ref[2:3, :]
    is_image = slot >= 0
    low, span = qpos_ref[0:1, :], qpos_ref[1:2, :]
    item = lax.broadcasted_iota(jnp.int32, (shared.shape[0], 1), 0)
    placed = dot0(shared, jnp.where(item == slot, 1.0, 0.0).astype(BF16))
    input_ref[...] = jnp.where(
        is_image, placed[INPUT_AT:PLACE_AT], text_ref[...].astype(F32)
    ).astype(BF16)
    query = jnp.where(is_image, placed[:HEAD_DIM].astype(BF16), text_q_ref[:HEAD_DIM])
    query_ref[:HEAD_DIM] = query
    query_ref[HEAD_DIM:] = text_q_ref[HEAD_DIM:]
    place = shared[:, PLACE_AT : PLACE_AT + 2].astype(F32).astype(jnp.int32)
    key_pos = place[:, :1] * 64 + place[:, 1:]
    keys = shared[:, KEY_AT : KEY_AT + HEAD_DIM]
    scores = jnp.dot(keys, query, preferred_element_type=F32)
    factor = LOG2E * HEAD_DIM ** (-0.5)
    offset = key_pos - low
    scores = jnp.where((offset >= 0) & (offset <= span), scores, NEG)
    best = jnp.where(is_image, NEG, text_stat_ref[0:1, :])
    new_best = jnp.maximum(best, jnp.max(scores, axis=0, keepdims=True))
    weights = jnp.exp2((scores - new_best) * factor)
    keep = jnp.where(is_image, 0.0, jnp.exp2((best - new_best) * factor))
    stat_ref[0:1, :] = new_best
    stat_ref[1:2, :] = text_stat_ref[1:2, :] * keep + jnp.sum(weights, axis=0, keepdims=True)
    added = dot0(shared, weights.astype(BF16))[VALUE_AT:INPUT_AT]
    mix_ref[...] = text_mix_ref[...] * keep + added
    tiles = busy_ref.shape[0]
    width = slot.shape[1] // tiles
    for tile in range(tiles):
        lanes = slice(tile * width, (tile + 1) * width)

        @pl.when(busy_ref[tile] > 0)
        def _():
            best, total, mixed = fold_text(
                bounds_ref,
                kv_ref,
                (stat_ref[0:1, lanes], stat_ref[1:2, lanes], mix_ref[:, lanes]),
                query_ref[:, lanes],
                qpos_ref[0:1, lanes],
                qpos_ref[1:2, lanes],
                qpos_ref[2:3, lanes] >= 0,
            )
            stat_ref[0:1, lanes] = best
            stat_ref[1:2, lanes] = total
            mix_ref[:, lanes] = mixed

    out_ref[...] = (mix_ref[...] / stat_ref[1:2, :]).astype(BF16)


def attention_params():
    return pltpu.CompilerParams(vmem_limit_bytes=24 * 1024 * 1024)


def text_attention(bounds, query, keyval, qpos):
    vmem = pl.BlockSpec(memory_space=pltpu.VMEM)
    count = query.shape[1]
    pairs = count * keyval.shape[0] * keyval.shape[1] * keyval.shape[3]
    return pl.pallas_call(
        text_kernel,
        out_shape=(
            jax.ShapeDtypeStruct((HEAD_DIM, count), F32),
            jax.ShapeDtypeStruct((8, count), F32),
        ),
        in_specs=[pl.BlockSpec(memory_space=pltpu.SMEM)] + [vmem] * 3,
        out_specs=(vmem, vmem),
        compiler_params=attention_params(),
        cost_estimate=pl.CostEstimate(
            flops=4 * HEAD_DIM * pairs, bytes_accessed=2 * keyval.size, transcendentals=pairs
        ),
        name="text_attention",
    )(bounds, query, keyval, qpos)


def image_attention(bounds, busy, shared, text, text_query, keyval, qpos, mixed, stats):
    vmem = pl.BlockSpec(memory_space=pltpu.VMEM)
    count = text.shape[1]
    return pl.pallas_call(
        image_kernel,
        out_shape=(
            jax.ShapeDtypeStruct((HEAD_DIM, count), BF16),
            jax.ShapeDtypeStruct((HEAD_DIM, count), BF16),
        ),
        in_specs=[pl.BlockSpec(memory_space=pltpu.SMEM)] * 2 + [vmem] * 7,
        out_specs=(vmem, vmem),
        scratch_shapes=[
            pltpu.VMEM(text_query.shape, BF16),
            pltpu.VMEM((HEAD_DIM, count), F32),
            pltpu.VMEM((8, count), F32),
        ],
        compiler_params=attention_params(),
        name="image_attention",
    )(bounds, busy, shared, text, text_query, keyval, qpos, mixed, stats)


def vision_kernel(part, pitch, ends_ref, q_ref, kv_ref, marks_ref, out_ref):
    keyval = kv_ref[...]
    scores = lax.dot_general(
        keyval, q_ref[...], (((1,), (1,)), ((), ())), preferred_element_type=F32
    ) * (HEAD_DIM ** (-0.5))
    count = q_ref.shape[0]
    item = lax.broadcasted_iota(jnp.int32, (keyval.shape[0], 1), 0)
    inner = item % count
    merged = (inner // part * pitch + item // count * part + inner % part) // 4
    marks = jnp.zeros_like(merged)
    for index in range(ends_ref.shape[0]):
        marks = marks + (merged >= ends_ref[index]).astype(jnp.int32)
    allowed = marks == marks_ref[...]
    scores = jnp.where(allowed, scores, NEG)
    best = jnp.max(scores, axis=0, keepdims=True)
    weights = jnp.where(allowed, jnp.exp(scores - best), 0.0)
    total = jnp.sum(weights, axis=0, keepdims=True)
    mixed = dot0(keyval, weights.astype(BF16))[HEAD_DIM:]
    out_ref[...] = jnp.broadcast_to((mixed / total).astype(BF16)[None], out_ref.shape)


def vision_attention(part, pitch, copies, ends, query, keyval, marks):
    vmem = pl.BlockSpec(memory_space=pltpu.VMEM)
    return pl.pallas_call(
        functools.partial(vision_kernel, part, pitch),
        out_shape=jax.ShapeDtypeStruct((copies, HEAD_DIM, query.shape[0]), BF16),
        in_specs=[pl.BlockSpec(memory_space=pltpu.SMEM)] + [vmem] * 3,
        out_specs=vmem,
        compiler_params=pltpu.CompilerParams(vmem_limit_bytes=16 * 1024 * 1024),
        name="vision_attention",
    )(ends, query, keyval, marks)


def per_device(
    patches,
    vis_gain,
    vis_bias,
    vis_qkv,
    vis_qkv_bias,
    vis_out,
    vis_out_bias,
    proj_weight,
    proj_bias,
    text_embeds,
    dec_gain,
    dec_qkv,
    dec_out,
    image_tokens,
    text_gaps,
    doc_lengths,
):
    cols = lax.axis_size("col")
    rows = lax.axis_size("row")
    row = lax.axis_index("row")
    col = lax.axis_index("col")
    half = lax.axis_index("grp")

    feat_c = vis_out.shape[1]
    vis_n = vis_qkv.shape[1]
    unit = -(-(vis_n + HEAD_DIM) // 128) * 128
    fill = jnp.zeros((HEAD_DIM, unit - vis_n - HEAD_DIM), BF16)
    sides = (slice(0, HEAD_DIM), slice(HEAD_DIM, 2 * HEAD_DIM))
    units = [
        [dec_qkv[:, at * vis_n : (at + 1) * vis_n], vis_out[:, side], fill]
        for at, side in enumerate(sides)
    ]
    units += [[vis_qkv[side], dec_out[side], fill] for side in sides]
    units += [[proj_weight[window, side] for window in range(4)] + [fill] for side in sides]
    packed = jnp.stack([jnp.concatenate(pieces, axis=1) for pieces in units])
    gathered_w = lax.all_gather(packed, "col", axis=0)

    def pair(number):
        return lax.slice_in_dim(gathered_w, 2 * number, 2 * number + 2, axis=1)

    rows_b = patches.shape[1]
    part = rows_b // cols
    affine_own = jnp.stack([vis_gain, vis_bias, vis_out_bias])
    affine_own = jnp.pad(affine_own, ((0, 8 - affine_own.shape[0]), (0, 0)))
    mine = exchange(
        jnp.concatenate(
            [
                patches[0].reshape(cols, part, feat_c),
                jnp.broadcast_to(affine_own[None], (cols, 8, feat_c)),
            ],
            axis=1,
        ),
        "col",
    )
    mine = jnp.transpose(mine, (1, 0, 2)).reshape(part + 8, WIDTH)
    affine = mine[part : part + 3].astype(F32)

    text = text_embeds[0].T
    positions = text.shape[1]
    folds = -(-(WIDTH + HEAD_DIM) // positions)
    spare = folds * positions - WIDTH
    gain = jnp.broadcast_to(jnp.pad(dec_gain, (0, spare - HEAD_DIM))[None], (part, spare))
    folded = jnp.concatenate([mine[:part], gain], axis=1)
    folded = jnp.transpose(folded.reshape(part, folds, positions), (1, 0, 2))
    both = spread(
        jnp.concatenate([text, folded.reshape(folds * part, positions)], axis=0), "row"
    )
    text_all = both[:, :HEAD_DIM].reshape(WIDTH, positions)
    raw = jnp.transpose(
        both[:, HEAD_DIM:].reshape(rows, folds, part, positions), (0, 2, 1, 3)
    ).reshape(rows, part, folds * positions)
    gain_all = raw[:, 0, WIDTH : WIDTH + HEAD_DIM].reshape(WIDTH, 1).astype(F32)
    raw = raw[:, :, :WIDTH].reshape(rows * part, WIDTH)

    row_pack, gathered_w = lax.optimization_barrier((pair(0), gathered_w))
    row_w = exchange(row_pack.reshape(rows, HEAD_DIM, unit), "row").reshape(WIDTH, unit)

    vis_w = pair(1).reshape(WIDTH, unit)
    xfull = raw.astype(F32)
    mean = jnp.sum(xfull, axis=1, keepdims=True) / WIDTH
    variance = jnp.sum(xfull * xfull, axis=1, keepdims=True) / WIDTH - mean * mean
    normed = (
        (xfull - mean) * lax.rsqrt(variance + 1e-06) * affine[0:1] + affine[1:2]
    ).astype(BF16)
    qkv_rows = (
        jnp.dot(normed, vis_w, preferred_element_type=F32)[:, :vis_n]
        + vis_qkv_bias.astype(F32)
    ).astype(BF16)
    text_all, qkv_rows = lax.optimization_barrier((text_all, qkv_rows))
    xtext = text_all.astype(F32)
    squares = jnp.sum(xtext * xtext, axis=0, keepdims=True)
    text_normed = (xtext * lax.rsqrt(squares / WIDTH + 1e-05) * gain_all).astype(BF16)
    count = rows * part
    query = qkv_rows[:, :HEAD_DIM]
    lengths, gaps = image_tokens[0], text_gaps[0]
    own_rows = col * positions + jnp.arange(positions, dtype=jnp.int32)
    source, inside = insert_map(own_rows, lengths, gaps)
    query_pos = sequence_position(own_rows, half)
    ends = running(doc_lengths)
    low = jnp.max(
        jnp.where(query_pos[:, None] >= ends[None, :], ends[None, :], 0), axis=1
    )
    bounds = jnp.stack([jnp.min(low) // (2 * positions), col + 1]).astype(jnp.int32)
    merged = count // 4
    pack = part // 4
    item = jnp.arange(merged, dtype=jnp.int32)
    merged_id = item // pack * (pack * cols) + col * pack + item % pack
    marks = jnp.tile(segment_of(merged_id, lengths), 4)[None]
    image_ends = running(lengths)
    place = sequence_position(rows_of_merged(merged_id, lengths, gaps), half)
    place = jnp.stack([place // 64, place % 64], axis=1).astype(BF16)
    slot = (source // pack % cols * 2 + half) * merged
    slot = slot + source // (pack * cols) * pack + source % pack
    slot = jnp.where(inside, slot, -1)
    qpos = jnp.stack([low, query_pos - low, slot])
    busy = jnp.max(inside.astype(jnp.int32).reshape(4, positions // 4), axis=1)
    bias = jnp.where(inside, NEG, 0.0).astype(BF16)[None]
    row_w, vis_kv, qpos, bounds, marks, image_ends, place, busy, bias = (
        lax.optimization_barrier(
            (
                row_w,
                qkv_rows[:, HEAD_DIM:],
                qpos,
                bounds,
                marks,
                image_ends,
                place,
                busy,
                bias,
            )
        )
    )
    keyval = spread(vis_kv, "col").reshape(cols * count, 2 * HEAD_DIM)
    proj_w = pair(2).reshape(WIDTH, unit)
    dec_out_w = vis_w[:, vis_n : vis_n + HEAD_DIM]

    text_qkv = dot0(row_w, text_normed)[:vis_n].astype(BF16)
    own_kv = jnp.concatenate(
        [
            text_qkv[HEAD_DIM : 2 * HEAD_DIM],
            jnp.pad(bias, ((0, 7), (0, 0))),
            text_qkv[2 * HEAD_DIM :],
        ],
        axis=0,
    )
    other_kv = lax.ppermute(own_kv, "grp", [(0, 1), (1, 0)])
    pair_kv = jnp.where(half == 0, jnp.stack([own_kv, other_kv]), jnp.stack([other_kv, own_kv]))
    pair_kv, keyval = lax.optimization_barrier((pair_kv, keyval))
    all_kv = lax.all_gather(pair_kv, "col", axis=0)

    def window_first(array):
        features = array.shape[1]
        return jnp.transpose(
            array.reshape(rows, part // 4, 4, features), (2, 0, 1, 3)
        ).reshape(count, features)

    query = jnp.pad(window_first(query), ((0, 0), (0, HEAD_DIM)))
    all_attn = exchange(
        vision_attention(part, rows_b, rows, image_ends, query, keyval, marks), "row"
    ).reshape(WIDTH, count)
    raw_at = row * HEAD_DIM
    own_raw = window_first(lax.dynamic_slice(raw, (0, raw_at), (count, HEAD_DIM)))
    own_bias = lax.dynamic_slice(affine[2], (raw_at,), (HEAD_DIM,))
    resid = (own_raw.T.astype(F32) + dot0(row_w, all_attn)[vis_n : vis_n + HEAD_DIM] + own_bias[:, None]).astype(BF16)
    all_resid = spread(resid, "row").reshape(WIDTH, count)
    windows = dot0(proj_w, all_resid)
    projected = proj_bias.astype(F32)[:, None]
    for window in range(4):
        projected = projected + windows[
            window * HEAD_DIM : (window + 1) * HEAD_DIM, window * merged : (window + 1) * merged
        ]
    image_in = projected.T.astype(BF16)

    image_all = jnp.transpose(spread(image_in, "row"), (1, 0, 2)).reshape(merged, WIDTH)
    ximage = image_all.astype(F32)
    squares = jnp.sum(ximage * ximage, axis=1, keepdims=True)
    image_normed = (
        ximage * lax.rsqrt(squares / WIDTH + 1e-05) * gain_all[:, 0][None, :]
    ).astype(BF16)
    all_kv, image_normed = lax.optimization_barrier((all_kv, image_normed))
    image_qkv = jnp.dot(image_normed, row_w, preferred_element_type=F32)[:, :vis_n].astype(BF16)

    def with_mask_row(query):
        return jnp.concatenate(
            [query, jnp.ones((1, positions), BF16), jnp.zeros((7, positions), BF16)], axis=0
        )

    text_query = with_mask_row(text_qkv[:HEAD_DIM])
    mixed, stats = text_attention(bounds, text_query, all_kv, qpos)
    shared = spread(
        jnp.concatenate(
            [
                image_qkv[:, : 2 * HEAD_DIM],
                jnp.zeros((merged, 8), BF16),
                image_qkv[:, 2 * HEAD_DIM :],
                image_in,
                place,
            ],
            axis=1,
        ),
        ("col", "grp"),
    )
    shared, mixed = lax.optimization_barrier((shared, mixed))
    shared = shared.reshape(cols * 2 * merged, -1)
    dec_attn, dec_input = image_attention(
        bounds, busy, shared, text, text_query, all_kv, qpos, mixed, stats
    )

    all_dec = spread(dec_attn, "row").reshape(WIDTH, positions)
    delta = dot0(dec_out_w, all_dec)
    return (dec_input.astype(F32) + delta).astype(BF16).T[None]


def solution(mesh):
    return jax.shard_map(
        per_device,
        mesh=mesh,
        in_specs=(
            P("grp", "row", "col"),
            P("col"),
            P("col"),
            P("col", "row"),
            P("row"),
            P("row", "col"),
            P("col"),
            P(None, "col", "row"),
            P("row"),
            P("grp", "col", "row"),
            P("row"),
            P("row", "col"),
            P("col", "row"),
            P("grp", None),
            P("grp", None),
            P(),
        ),
        out_specs=P("grp", "col", "row"),
        check_vma=False,
    )
```

```python
import functools

import jax
import jax.numpy as jnp
from jax import lax
from jax.experimental import pallas as pl
from jax.experimental.pallas import tpu as pltpu
from jax.sharding import PartitionSpec as P

HEADS = 16
HEAD_DIM = 88
WIDTH = HEADS * HEAD_DIM
TPD = 256
LOG2E = 1.4426950408889634
NEG = -1e30
F32 = jnp.float32
BF16 = jnp.bfloat16


def spread(values, axes):
    count = lax.axis_size(axes)
    return lax.all_to_all(
        jnp.broadcast_to(values[None], (count,) + values.shape), axes, split_axis=0, concat_axis=0
    )


def exchange(values, axes):
    return lax.all_to_all(values, axes, split_axis=0, concat_axis=0)


def dot0(left, right):
    return lax.dot_general(left, right, (((0,), (0,)), ((), ())), preferred_element_type=F32)


def running(lengths):
    at = jnp.arange(lengths.shape[0], dtype=jnp.int32)
    return jnp.sum(
        jnp.where(at[None, :] <= at[:, None], lengths[None, :], 0), axis=1, dtype=jnp.int32
    )


def segment_of(index_values, lengths):
    ends = running(lengths)
    return jnp.sum(
        (index_values[:, None] >= ends[None, :]).astype(jnp.int32), axis=1, dtype=jnp.int32
    )


def image_starts(lengths, gaps):
    offsets = running(lengths) - lengths
    return running(gaps)[: lengths.shape[0]] + offsets, offsets


def insert_map(text_rows, lengths, gaps):
    starts, offsets = image_starts(lengths, gaps)
    inside = (text_rows[:, None] >= starts[None, :]) & (
        text_rows[:, None] < (starts + lengths)[None, :]
    )
    source = jnp.sum(
        jnp.where(inside, offsets[None, :] + text_rows[:, None] - starts[None, :], 0),
        axis=1,
        dtype=jnp.int32,
    )
    return source, jnp.any(inside, axis=1)


def rows_of_merged(merged, lengths, gaps):
    starts, offsets = image_starts(lengths, gaps)
    inside = (merged[:, None] >= offsets[None, :]) & (
        merged[:, None] < (offsets + lengths)[None, :]
    )
    return jnp.sum(
        jnp.where(inside, starts[None, :] + merged[:, None] - offsets[None, :], 0),
        axis=1,
        dtype=jnp.int32,
    )


def sequence_position(rows, half):
    return (rows // TPD) * (2 * TPD) + half * TPD + rows % TPD


def fold_block(state, query, keys, values, key_pos, low, span):
    best, total, mixed = state
    factor = LOG2E * HEAD_DIM ** (-0.5)
    scores = dot0(keys, query)
    offset = key_pos - low
    allowed = (offset >= 0) & (offset <= span)
    scores = jnp.where(allowed, scores, NEG)
    new_best = jnp.maximum(best, jnp.max(scores, axis=0, keepdims=True))
    weights = jnp.exp2((scores - new_best) * factor)
    keep = jnp.exp2((best - new_best) * factor)
    total = total * keep + jnp.sum(weights, axis=0, keepdims=True)
    added = jnp.dot(values, weights.astype(BF16), preferred_element_type=F32)
    return new_best, total, mixed * keep + added


def fold_text(bounds_ref, kv_ref, state, query, low, span):
    block = kv_ref.shape[3]
    key_rows = query.shape[0]
    step = lax.broadcasted_iota(jnp.int32, (block, 1), 0)
    in_pair = jnp.where(step >= TPD, step + TPD, step)

    def chunk(index, state):
        for half in range(2):
            keys = kv_ref[index, half, :key_rows]
            values = kv_ref[index, half, key_rows:]
            key_pos = in_pair + (index * (2 * block) + half * TPD)
            state = fold_block(state, query, keys, values, key_pos, low, span)
        return state

    return lax.fori_loop(bounds_ref[0], bounds_ref[1], chunk, state)


def text_kernel(bounds_ref, q_ref, kv_ref, qpos_ref, mix_ref, stat_ref):
    count = q_ref.shape[1]
    state = (
        jnp.full((1, count), NEG, F32),
        jnp.zeros((1, count), F32),
        jnp.zeros((HEAD_DIM, count), F32),
    )
    best, total, mixed = fold_text(
        bounds_ref, kv_ref, state, q_ref[...], qpos_ref[0:1, :], qpos_ref[1:2, :]
    )
    stat_ref[0:1, :] = best
    stat_ref[1:2, :] = total
    mix_ref[...] = mixed


KEY_AT = HEAD_DIM
VALUE_AT = 2 * HEAD_DIM + 8
INPUT_AT = VALUE_AT + HEAD_DIM
PLACE_AT = INPUT_AT + HEAD_DIM


KEY_AT = HEAD_DIM
VALUE_AT = 2 * HEAD_DIM + 8
INPUT_AT = VALUE_AT + HEAD_DIM
PLACE_AT = INPUT_AT + HEAD_DIM
TILE = 128


def image_kernel(
    bounds_ref,
    shared_ref,
    text_ref,
    text_q_ref,
    kv_ref,
    qpos_ref,
    packed_ref,
    text_mix_ref,
    text_stat_ref,
    out_ref,
    input_ref,
    found_ref,
):
    shared = shared_ref[...]
    place = shared[:, PLACE_AT : PLACE_AT + 2].astype(F32).astype(jnp.int32)
    key_pos = place[:, :1] * 64 + place[:, 1:]
    keys = jnp.concatenate(
        [shared[:, KEY_AT : KEY_AT + HEAD_DIM].T, jnp.zeros((8, shared.shape[0]), BF16)], axis=0
    )
    values = shared[:, VALUE_AT:INPUT_AT].T
    state = (text_stat_ref[0:1, :], text_stat_ref[1:2, :], text_mix_ref[...])
    best, total, mixed = fold_block(
        state, text_q_ref[...], keys, values, key_pos, qpos_ref[0:1, :], qpos_ref[1:2, :]
    )
    mixed = (mixed / total).astype(BF16)

    found_ref[...] = jnp.zeros_like(found_ref)
    item = lax.broadcasted_iota(jnp.int32, (shared.shape[0], 1), 0)
    for tile in range(packed_ref.shape[1] // TILE):
        lanes = slice(tile * TILE, (tile + 1) * TILE)

        @pl.when(bounds_ref[2] > tile * TILE)
        def _():
            low, span = packed_ref[0:1, lanes], packed_ref[1:2, lanes]
            slot = packed_ref[2:3, lanes]
            placed = dot0(shared, jnp.where(item == slot, 1.0, 0.0).astype(BF16)).astype(BF16)
            query = jnp.concatenate([placed[:HEAD_DIM], text_q_ref[HEAD_DIM:, :TILE]], axis=0)
            state = (
                jnp.full((1, TILE), NEG, F32),
                jnp.zeros((1, TILE), F32),
                jnp.zeros((HEAD_DIM, TILE), F32),
            )
            state = fold_block(state, query, keys, values, key_pos, low, span)
            best, total, mixed = fold_text(bounds_ref, kv_ref, state, query, low, span)
            found_ref[:HEAD_DIM, lanes] = (mixed / total).astype(BF16)
            found_ref[HEAD_DIM:, lanes] = placed[INPUT_AT:PLACE_AT]

    rank = qpos_ref[2:3, :]
    spot = lax.broadcasted_iota(jnp.int32, (packed_ref.shape[1], 1), 0)
    spread_out = jnp.dot(
        found_ref[...], jnp.where(spot == rank, 1.0, 0.0).astype(BF16), preferred_element_type=F32
    ).astype(BF16)
    is_image = rank >= 0
    out_ref[...] = jnp.where(is_image, spread_out[:HEAD_DIM], mixed)
    input_ref[...] = jnp.where(is_image, spread_out[HEAD_DIM:], text_ref[...])


def attention_params():
    return pltpu.CompilerParams(vmem_limit_bytes=24 * 1024 * 1024)


def text_attention(bounds, query, keyval, qpos):
    vmem = pl.BlockSpec(memory_space=pltpu.VMEM)
    count = query.shape[1]
    pairs = count * keyval.shape[0] * keyval.shape[1] * keyval.shape[3]
    return pl.pallas_call(
        text_kernel,
        out_shape=(
            jax.ShapeDtypeStruct((HEAD_DIM, count), F32),
            jax.ShapeDtypeStruct((8, count), F32),
        ),
        in_specs=[pl.BlockSpec(memory_space=pltpu.SMEM)] + [vmem] * 3,
        out_specs=(vmem, vmem),
        compiler_params=attention_params(),
        cost_estimate=pl.CostEstimate(
            flops=4 * HEAD_DIM * pairs, bytes_accessed=2 * keyval.size, transcendentals=pairs
        ),
        name="text_attention",
    )(bounds, query, keyval, qpos)


def image_attention(bounds, shared, text, text_query, keyval, qpos, packed, mixed, stats):
    vmem = pl.BlockSpec(memory_space=pltpu.VMEM)
    count = text.shape[1]
    return pl.pallas_call(
        image_kernel,
        out_shape=(
            jax.ShapeDtypeStruct((HEAD_DIM, count), BF16),
            jax.ShapeDtypeStruct((HEAD_DIM, count), BF16),
        ),
        in_specs=[pl.BlockSpec(memory_space=pltpu.SMEM)] + [vmem] * 8,
        out_specs=(vmem, vmem),
        scratch_shapes=[pltpu.VMEM((2 * HEAD_DIM, packed.shape[1]), BF16)],
        compiler_params=attention_params(),
        name="image_attention",
    )(bounds, shared, text, text_query, keyval, qpos, packed, mixed, stats)


def vision_kernel(part, pitch, ends_ref, q_ref, kv_ref, marks_ref, out_ref):
    keyval = kv_ref[...]
    scores = lax.dot_general(
        keyval, q_ref[...], (((1,), (1,)), ((), ())), preferred_element_type=F32
    ) * (HEAD_DIM ** (-0.5))
    count = q_ref.shape[0]
    item = lax.broadcasted_iota(jnp.int32, (keyval.shape[0], 1), 0)
    inner = item % count
    merged = (inner // part * pitch + item // count * part + inner % part) // 4
    marks = jnp.zeros_like(merged)
    for index in range(ends_ref.shape[0]):
        marks = marks + (merged >= ends_ref[index]).astype(jnp.int32)
    allowed = marks == marks_ref[...]
    scores = jnp.where(allowed, scores, NEG)
    best = jnp.max(scores, axis=0, keepdims=True)
    weights = jnp.where(allowed, jnp.exp(scores - best), 0.0)
    total = jnp.sum(weights, axis=0, keepdims=True)
    mixed = dot0(keyval, weights.astype(BF16))[HEAD_DIM:]
    out_ref[...] = jnp.broadcast_to((mixed / total).astype(BF16)[None], out_ref.shape)


def vision_attention(part, pitch, copies, ends, query, keyval, marks):
    vmem = pl.BlockSpec(memory_space=pltpu.VMEM)
    return pl.pallas_call(
        functools.partial(vision_kernel, part, pitch),
        out_shape=jax.ShapeDtypeStruct((copies, HEAD_DIM, query.shape[0]), BF16),
        in_specs=[pl.BlockSpec(memory_space=pltpu.SMEM)] + [vmem] * 3,
        out_specs=vmem,
        compiler_params=pltpu.CompilerParams(vmem_limit_bytes=16 * 1024 * 1024),
        name="vision_attention",
    )(ends, query, keyval, marks)


def per_device(
    patches,
    vis_gain,
    vis_bias,
    vis_qkv,
    vis_qkv_bias,
    vis_out,
    vis_out_bias,
    proj_weight,
    proj_bias,
    text_embeds,
    dec_gain,
    dec_qkv,
    dec_out,
    image_tokens,
    text_gaps,
    doc_lengths,
):
    cols = lax.axis_size("col")
    rows = lax.axis_size("row")
    row = lax.axis_index("row")
    col = lax.axis_index("col")
    half = lax.axis_index("grp")

    feat_c = vis_out.shape[1]
    vis_n = vis_qkv.shape[1]
    unit = -(-(vis_n + HEAD_DIM) // 128) * 128
    fill = jnp.zeros((HEAD_DIM, unit - vis_n - HEAD_DIM), BF16)
    sides = (slice(0, HEAD_DIM), slice(HEAD_DIM, 2 * HEAD_DIM))
    units = [
        [dec_qkv[:, at * vis_n : (at + 1) * vis_n], vis_out[:, side], fill]
        for at, side in enumerate(sides)
    ]
    units += [[vis_qkv[side], dec_out[side], fill] for side in sides]
    units += [[proj_weight[window, side] for window in range(4)] + [fill] for side in sides]
    packed = jnp.stack([jnp.concatenate(pieces, axis=1) for pieces in units])
    gathered_w = lax.all_gather(packed, "col", axis=0)

    def pair(number):
        return lax.slice_in_dim(gathered_w, 2 * number, 2 * number + 2, axis=1)

    rows_b = patches.shape[1]
    part = rows_b // cols
    affine_own = jnp.stack([vis_gain, vis_bias, vis_out_bias])
    affine_own = jnp.pad(affine_own, ((0, 8 - affine_own.shape[0]), (0, 0)))
    mine = exchange(
        jnp.concatenate(
            [
                patches[0].reshape(cols, part, feat_c),
                jnp.broadcast_to(affine_own[None], (cols, 8, feat_c)),
            ],
            axis=1,
        ),
        "col",
    )
    mine = jnp.transpose(mine, (1, 0, 2)).reshape(part + 8, WIDTH)
    affine = mine[part : part + 3].astype(F32)

    text = text_embeds[0].T
    positions = text.shape[1]
    folds = -(-(WIDTH + HEAD_DIM) // positions)
    spare = folds * positions - WIDTH
    gain = jnp.broadcast_to(jnp.pad(dec_gain, (0, spare - HEAD_DIM))[None], (part, spare))
    folded = jnp.concatenate([mine[:part], gain], axis=1)
    folded = jnp.transpose(folded.reshape(part, folds, positions), (1, 0, 2))
    both = spread(
        jnp.concatenate([text, folded.reshape(folds * part, positions)], axis=0), "row"
    )
    text_all = both[:, :HEAD_DIM].reshape(WIDTH, positions)
    raw = jnp.transpose(
        both[:, HEAD_DIM:].reshape(rows, folds, part, positions), (0, 2, 1, 3)
    ).reshape(rows, part, folds * positions)
    gain_all = raw[:, 0, WIDTH : WIDTH + HEAD_DIM].reshape(WIDTH, 1).astype(F32)
    raw = raw[:, :, :WIDTH].reshape(rows * part, WIDTH)

    row_pack, gathered_w = lax.optimization_barrier((pair(0), gathered_w))
    row_w = exchange(row_pack.reshape(rows, HEAD_DIM, unit), "row").reshape(WIDTH, unit)

    vis_w = pair(1).reshape(WIDTH, unit)
    xfull = raw.astype(F32)
    mean = jnp.sum(xfull, axis=1, keepdims=True) / WIDTH
    variance = jnp.sum(xfull * xfull, axis=1, keepdims=True) / WIDTH - mean * mean
    normed = (
        (xfull - mean) * lax.rsqrt(variance + 1e-06) * affine[0:1] + affine[1:2]
    ).astype(BF16)
    qkv_rows = (
        jnp.dot(normed, vis_w, preferred_element_type=F32)[:, :vis_n]
        + vis_qkv_bias.astype(F32)
    ).astype(BF16)
    text_all, qkv_rows = lax.optimization_barrier((text_all, qkv_rows))
    xtext = text_all.astype(F32)
    squares = jnp.sum(xtext * xtext, axis=0, keepdims=True)
    text_normed = (xtext * lax.rsqrt(squares / WIDTH + 1e-05) * gain_all).astype(BF16)
    count = rows * part
    query = qkv_rows[:, :HEAD_DIM]
    lengths, gaps = image_tokens[0], text_gaps[0]
    own_rows = col * positions + jnp.arange(positions, dtype=jnp.int32)
    source, inside = insert_map(own_rows, lengths, gaps)
    query_pos = sequence_position(own_rows, half)
    ends = running(doc_lengths)
    low = jnp.max(
        jnp.where(query_pos[:, None] >= ends[None, :], ends[None, :], 0), axis=1
    )
    merged = count // 4
    pack = part // 4
    item = jnp.arange(merged, dtype=jnp.int32)
    merged_id = item // pack * (pack * cols) + col * pack + item % pack
    marks = jnp.tile(segment_of(merged_id, lengths), 4)[None]
    image_ends = running(lengths)
    place = sequence_position(rows_of_merged(merged_id, lengths, gaps), half)
    place = jnp.stack([place // 64, place % 64], axis=1).astype(BF16)
    total_merged = cols * merged
    first = jnp.min(jnp.where(inside, source, total_merged))
    found = jnp.sum(inside.astype(jnp.int32), dtype=jnp.int32)
    rank = jnp.where(inside, source - first, -1)
    near = jnp.arange(total_merged, dtype=jnp.int32)
    row_of = first + near
    slot = (row_of // pack % cols * 2 + half) * merged
    slot = slot + row_of // (pack * cols) * pack + row_of % pack
    near_pos = sequence_position(rows_of_merged(row_of, lengths, gaps), half)
    near_low = jnp.max(jnp.where(near_pos[:, None] >= ends[None, :], ends[None, :], 0), axis=1)
    packed = jnp.stack([near_low, near_pos - near_low, jnp.where(near < found, slot, -1)])
    qpos = jnp.stack([low, query_pos - low, rank])
    bounds = jnp.stack([jnp.min(low) // (2 * positions), col + 1, found]).astype(jnp.int32)
    bias = jnp.where(inside, NEG, 0.0).astype(BF16)[None]
    row_w, vis_kv, qpos, bounds, marks, image_ends, place, packed, bias = (
        lax.optimization_barrier(
            (
                row_w,
                qkv_rows[:, HEAD_DIM:],
                qpos,
                bounds,
                marks,
                image_ends,
                place,
                packed,
                bias,
            )
        )
    )
    keyval = spread(vis_kv, "col").reshape(cols * count, 2 * HEAD_DIM)
    proj_w = pair(2).reshape(WIDTH, unit)
    dec_out_w = vis_w[:, vis_n : vis_n + HEAD_DIM]

    text_qkv = dot0(row_w, text_normed)[:vis_n].astype(BF16)
    own_kv = jnp.concatenate(
        [
            text_qkv[HEAD_DIM : 2 * HEAD_DIM],
            jnp.pad(bias, ((0, 7), (0, 0))),
            text_qkv[2 * HEAD_DIM :],
        ],
        axis=0,
    )
    other_kv = lax.ppermute(own_kv, "grp", [(0, 1), (1, 0)])
    pair_kv = jnp.where(half == 0, jnp.stack([own_kv, other_kv]), jnp.stack([other_kv, own_kv]))
    pair_kv, keyval = lax.optimization_barrier((pair_kv, keyval))
    all_kv = lax.all_gather(pair_kv, "col", axis=0)

    def window_first(array):
        features = array.shape[1]
        return jnp.transpose(
            array.reshape(rows, part // 4, 4, features), (2, 0, 1, 3)
        ).reshape(count, features)

    query = jnp.pad(window_first(query), ((0, 0), (0, HEAD_DIM)))
    all_attn = exchange(
        vision_attention(part, rows_b, rows, image_ends, query, keyval, marks), "row"
    ).reshape(WIDTH, count)
    raw_at = row * HEAD_DIM
    own_raw = window_first(lax.dynamic_slice(raw, (0, raw_at), (count, HEAD_DIM)))
    own_bias = lax.dynamic_slice(affine[2], (raw_at,), (HEAD_DIM,))
    resid = (own_raw.T.astype(F32) + dot0(row_w, all_attn)[vis_n : vis_n + HEAD_DIM] + own_bias[:, None]).astype(BF16)
    all_resid = spread(resid, "row").reshape(WIDTH, count)
    windows = dot0(proj_w, all_resid)
    projected = proj_bias.astype(F32)[:, None]
    for window in range(4):
        projected = projected + windows[
            window * HEAD_DIM : (window + 1) * HEAD_DIM, window * merged : (window + 1) * merged
        ]
    image_in = projected.T.astype(BF16)

    image_all = jnp.transpose(spread(image_in, "row"), (1, 0, 2)).reshape(merged, WIDTH)
    ximage = image_all.astype(F32)
    squares = jnp.sum(ximage * ximage, axis=1, keepdims=True)
    image_normed = (
        ximage * lax.rsqrt(squares / WIDTH + 1e-05) * gain_all[:, 0][None, :]
    ).astype(BF16)
    all_kv, image_normed = lax.optimization_barrier((all_kv, image_normed))
    image_qkv = jnp.dot(image_normed, row_w, preferred_element_type=F32)[:, :vis_n].astype(BF16)

    def with_mask_row(query):
        return jnp.concatenate(
            [query, jnp.ones((1, positions), BF16), jnp.zeros((7, positions), BF16)], axis=0
        )

    text_query = with_mask_row(text_qkv[:HEAD_DIM])
    mixed, stats = text_attention(bounds, text_query, all_kv, qpos)
    shared = spread(
        jnp.concatenate(
            [
                image_qkv[:, : 2 * HEAD_DIM],
                jnp.zeros((merged, 8), BF16),
                image_qkv[:, 2 * HEAD_DIM :],
                image_in,
                place,
            ],
            axis=1,
        ),
        ("col", "grp"),
    )
    shared, mixed = lax.optimization_barrier((shared, mixed))
    shared = shared.reshape(cols * 2 * merged, -1)
    dec_attn, dec_input = image_attention(
        bounds, shared, text, text_query, all_kv, qpos, packed, mixed, stats
    )

    all_dec = spread(dec_attn, "row").reshape(WIDTH, positions)
    delta = dot0(dec_out_w, all_dec)
    return (dec_input.astype(F32) + delta).astype(BF16).T[None]


def solution(mesh):
    return jax.shard_map(
        per_device,
        mesh=mesh,
        in_specs=(
            P("grp", "row", "col"),
            P("col"),
            P("col"),
            P("col", "row"),
            P("row"),
            P("row", "col"),
            P("col"),
            P(None, "col", "row"),
            P("row"),
            P("grp", "col", "row"),
            P("row"),
            P("row", "col"),
            P("col", "row"),
            P("grp", None),
            P("grp", None),
            P(),
        ),
        out_specs=P("grp", "col", "row"),
        check_vma=False,
    )
```

```python
import functools

import jax
import jax.numpy as jnp
from jax import lax
from jax.experimental import pallas as pl
from jax.experimental.pallas import tpu as pltpu
from jax.sharding import PartitionSpec as P

HEADS = 16
HEAD_DIM = 88
WIDTH = HEADS * HEAD_DIM
TPD = 256
LOG2E = 1.4426950408889634
NEG = -1e30
F32 = jnp.float32
BF16 = jnp.bfloat16


def spread(values, axes):
    count = lax.axis_size(axes)
    return lax.all_to_all(
        jnp.broadcast_to(values[None], (count,) + values.shape), axes, split_axis=0, concat_axis=0
    )


def exchange(values, axes):
    return lax.all_to_all(values, axes, split_axis=0, concat_axis=0)


def dot0(left, right):
    return lax.dot_general(left, right, (((0,), (0,)), ((), ())), preferred_element_type=F32)


def running(lengths):
    at = jnp.arange(lengths.shape[0], dtype=jnp.int32)
    return jnp.sum(
        jnp.where(at[None, :] <= at[:, None], lengths[None, :], 0), axis=1, dtype=jnp.int32
    )


def segment_of(index_values, lengths):
    ends = running(lengths)
    return jnp.sum(
        (index_values[:, None] >= ends[None, :]).astype(jnp.int32), axis=1, dtype=jnp.int32
    )


def image_starts(lengths, gaps):
    offsets = running(lengths) - lengths
    return running(gaps)[: lengths.shape[0]] + offsets, offsets


def insert_map(text_rows, lengths, gaps):
    starts, offsets = image_starts(lengths, gaps)
    inside = (text_rows[:, None] >= starts[None, :]) & (
        text_rows[:, None] < (starts + lengths)[None, :]
    )
    source = jnp.sum(
        jnp.where(inside, offsets[None, :] + text_rows[:, None] - starts[None, :], 0),
        axis=1,
        dtype=jnp.int32,
    )
    return source, jnp.any(inside, axis=1)


def rows_of_merged(merged, lengths, gaps):
    starts, offsets = image_starts(lengths, gaps)
    inside = (merged[:, None] >= offsets[None, :]) & (
        merged[:, None] < (offsets + lengths)[None, :]
    )
    return jnp.sum(
        jnp.where(inside, starts[None, :] + merged[:, None] - offsets[None, :], 0),
        axis=1,
        dtype=jnp.int32,
    )


def sequence_position(rows, half):
    return (rows // TPD) * (2 * TPD) + half * TPD + rows % TPD


def fold_block(state, query, keys, values, key_pos, low, span):
    best, total, mixed = state
    factor = LOG2E * HEAD_DIM ** (-0.5)
    scores = dot0(keys, query)
    offset = key_pos - low
    allowed = (offset >= 0) & (offset <= span)
    scores = jnp.where(allowed, scores, NEG)
    new_best = jnp.maximum(best, jnp.max(scores, axis=0, keepdims=True))
    weights = jnp.exp2((scores - new_best) * factor)
    keep = jnp.exp2((best - new_best) * factor)
    total = total * keep + jnp.sum(weights, axis=0, keepdims=True)
    added = jnp.dot(values, weights.astype(BF16), preferred_element_type=F32)
    return new_best, total, mixed * keep + added


def fold_text(bounds_ref, kv_ref, state, query, low, span):
    block = kv_ref.shape[3]
    key_rows = query.shape[0]
    step = lax.broadcasted_iota(jnp.int32, (block, 1), 0)
    in_pair = jnp.where(step >= TPD, step + TPD, step)

    def chunk(index, state):
        for half in range(2):
            keys = kv_ref[index, half, :key_rows]
            values = kv_ref[index, half, key_rows:]
            key_pos = in_pair + (index * (2 * block) + half * TPD)
            state = fold_block(state, query, keys, values, key_pos, low, span)
        return state

    return lax.fori_loop(bounds_ref[0], bounds_ref[1], chunk, state)


def text_kernel(bounds_ref, q_ref, kv_ref, qpos_ref, mix_ref, stat_ref):
    count = q_ref.shape[1]
    state = (
        jnp.full((1, count), NEG, F32),
        jnp.zeros((1, count), F32),
        jnp.zeros((HEAD_DIM, count), F32),
    )
    best, total, mixed = fold_text(
        bounds_ref, kv_ref, state, q_ref[...], qpos_ref[0:1, :], qpos_ref[1:2, :]
    )
    stat_ref[0:1, :] = best
    stat_ref[1:2, :] = total
    mix_ref[...] = mixed


KEY_AT = HEAD_DIM
VALUE_AT = 2 * HEAD_DIM + 8
INPUT_AT = VALUE_AT + HEAD_DIM
PLACE_AT = INPUT_AT + HEAD_DIM


KEY_AT = HEAD_DIM
VALUE_AT = 2 * HEAD_DIM + 8
INPUT_AT = VALUE_AT + HEAD_DIM
PLACE_AT = INPUT_AT + HEAD_DIM
TILE = 128


def image_kernel(
    bounds_ref,
    shared_ref,
    text_ref,
    text_q_ref,
    kv_ref,
    qpos_ref,
    packed_ref,
    text_mix_ref,
    text_stat_ref,
    out_ref,
    input_ref,
    found_ref,
):
    shared = shared_ref[...]
    place = shared[:, PLACE_AT : PLACE_AT + 2].astype(F32).astype(jnp.int32)
    key_pos = place[:, :1] * 64 + place[:, 1:]
    keys = jnp.concatenate(
        [shared[:, KEY_AT : KEY_AT + HEAD_DIM].T, jnp.zeros((8, shared.shape[0]), BF16)], axis=0
    )
    values = shared[:, VALUE_AT:INPUT_AT].T
    state = (text_stat_ref[0:1, :], text_stat_ref[1:2, :], text_mix_ref[...])
    best, total, mixed = fold_block(
        state, text_q_ref[...], keys, values, key_pos, qpos_ref[0:1, :], qpos_ref[1:2, :]
    )
    mixed = (mixed / total).astype(BF16)

    found_ref[...] = jnp.zeros_like(found_ref)
    item = lax.broadcasted_iota(jnp.int32, (shared.shape[0], 1), 0)
    for tile in range(packed_ref.shape[1] // TILE):
        lanes = slice(tile * TILE, (tile + 1) * TILE)

        @pl.when(bounds_ref[2] > tile * TILE)
        def _():
            low, span = packed_ref[0:1, lanes], packed_ref[1:2, lanes]
            slot = packed_ref[2:3, lanes]
            placed = dot0(shared, jnp.where(item == slot, 1.0, 0.0).astype(BF16)).astype(BF16)
            query = jnp.concatenate([placed[:HEAD_DIM], text_q_ref[HEAD_DIM:, :TILE]], axis=0)
            state = (
                jnp.full((1, TILE), NEG, F32),
                jnp.zeros((1, TILE), F32),
                jnp.zeros((HEAD_DIM, TILE), F32),
            )
            state = fold_block(state, query, keys, values, key_pos, low, span)
            best, total, mixed = fold_text(bounds_ref, kv_ref, state, query, low, span)
            found_ref[:HEAD_DIM, lanes] = (mixed / total).astype(BF16)
            found_ref[HEAD_DIM:, lanes] = placed[INPUT_AT:PLACE_AT]

    rank = qpos_ref[2:3, :]
    spot = lax.broadcasted_iota(jnp.int32, (packed_ref.shape[1], 1), 0)
    spread_out = jnp.dot(
        found_ref[...], jnp.where(spot == rank, 1.0, 0.0).astype(BF16), preferred_element_type=F32
    ).astype(BF16)
    is_image = rank >= 0
    out_ref[...] = jnp.where(is_image, spread_out[:HEAD_DIM], mixed)
    input_ref[...] = jnp.where(is_image, spread_out[HEAD_DIM:], text_ref[...])


def attention_params():
    return pltpu.CompilerParams(vmem_limit_bytes=24 * 1024 * 1024)


def text_attention(bounds, query, keyval, qpos):
    vmem = pl.BlockSpec(memory_space=pltpu.VMEM)
    count = query.shape[1]
    pairs = count * keyval.shape[0] * keyval.shape[1] * keyval.shape[3]
    return pl.pallas_call(
        text_kernel,
        out_shape=(
            jax.ShapeDtypeStruct((HEAD_DIM, count), F32),
            jax.ShapeDtypeStruct((8, count), F32),
        ),
        in_specs=[pl.BlockSpec(memory_space=pltpu.SMEM)] + [vmem] * 3,
        out_specs=(vmem, vmem),
        compiler_params=attention_params(),
        cost_estimate=pl.CostEstimate(
            flops=4 * HEAD_DIM * pairs, bytes_accessed=2 * keyval.size, transcendentals=pairs
        ),
        name="text_attention",
    )(bounds, query, keyval, qpos)


def image_attention(bounds, shared, text, text_query, keyval, qpos, packed, mixed, stats):
    vmem = pl.BlockSpec(memory_space=pltpu.VMEM)
    count = text.shape[1]
    return pl.pallas_call(
        image_kernel,
        out_shape=(
            jax.ShapeDtypeStruct((HEAD_DIM, count), BF16),
            jax.ShapeDtypeStruct((HEAD_DIM, count), BF16),
        ),
        in_specs=[pl.BlockSpec(memory_space=pltpu.SMEM)] + [vmem] * 8,
        out_specs=(vmem, vmem),
        scratch_shapes=[pltpu.VMEM((2 * HEAD_DIM, packed.shape[1]), BF16)],
        compiler_params=attention_params(),
        name="image_attention",
    )(bounds, shared, text, text_query, keyval, qpos, packed, mixed, stats)


def pack_kernel(
    dec_qkv_ref,
    vis_out_ref,
    vis_qkv_ref,
    dec_out_ref,
    proj_ref,
    patch_ref,
    gain_ref,
    bias_ref,
    out_bias_ref,
    out_ref,
    rows_ref,
):
    parts = rows_ref.shape[0]
    deep = patch_ref.shape[1] // parts
    affine = jnp.stack([gain_ref[...], bias_ref[...], out_bias_ref[...]])
    affine = jnp.concatenate([affine, jnp.zeros((5, affine.shape[1]), BF16)], axis=0)
    for at in range(parts):
        rows_ref[at, :deep] = patch_ref[0, at * deep : (at + 1) * deep]
        rows_ref[at, deep:] = affine
    width = vis_qkv_ref.shape[1]
    for at in range(2):
        side = slice(at * HEAD_DIM, (at + 1) * HEAD_DIM)
        fill = jnp.zeros((HEAD_DIM, out_ref.shape[2] - width - HEAD_DIM), BF16)
        out_ref[at, :, :width] = dec_qkv_ref[:, at * width : (at + 1) * width]
        out_ref[at, :, width : width + HEAD_DIM] = vis_out_ref[:, side]
        out_ref[at, :, width + HEAD_DIM :] = fill
        out_ref[2 + at, :, :width] = vis_qkv_ref[side]
        out_ref[2 + at, :, width : width + HEAD_DIM] = dec_out_ref[side]
        out_ref[2 + at, :, width + HEAD_DIM :] = fill
        for window in range(4):
            lanes = slice(window * HEAD_DIM, (window + 1) * HEAD_DIM)
            out_ref[4 + at, :, lanes] = proj_ref[window, side]
        out_ref[4 + at, :, 4 * HEAD_DIM :] = jnp.zeros(
            (HEAD_DIM, out_ref.shape[2] - 4 * HEAD_DIM), BF16
        )


def pack_arguments(unit, parts, *arrays):
    vmem = pl.BlockSpec(memory_space=pltpu.VMEM)
    return pl.pallas_call(
        pack_kernel,
        out_shape=(
            jax.ShapeDtypeStruct((6, HEAD_DIM, unit), BF16),
            jax.ShapeDtypeStruct(
                (parts, arrays[5].shape[1] // parts + 8, arrays[5].shape[2]), BF16
            ),
        ),
        in_specs=[vmem] * 9,
        out_specs=(vmem, vmem),
        compiler_params=pltpu.CompilerParams(vmem_limit_bytes=62 * 1024 * 1024),
        name="pack_arguments",
    )(*arrays)


def vision_kernel(part, pitch, ends_ref, q_ref, kv_ref, marks_ref, out_ref):
    keyval = kv_ref[...]
    scores = lax.dot_general(
        keyval, q_ref[...], (((1,), (1,)), ((), ())), preferred_element_type=F32
    ) * (HEAD_DIM ** (-0.5))
    count = q_ref.shape[0]
    item = lax.broadcasted_iota(jnp.int32, (keyval.shape[0], 1), 0)
    inner = item % count
    merged = (inner // part * pitch + item // count * part + inner % part) // 4
    marks = jnp.zeros_like(merged)
    for index in range(ends_ref.shape[0]):
        marks = marks + (merged >= ends_ref[index]).astype(jnp.int32)
    allowed = marks == marks_ref[...]
    scores = jnp.where(allowed, scores, NEG)
    best = jnp.max(scores, axis=0, keepdims=True)
    weights = jnp.where(allowed, jnp.exp(scores - best), 0.0)
    total = jnp.sum(weights, axis=0, keepdims=True)
    mixed = dot0(keyval, weights.astype(BF16))[HEAD_DIM:]
    out_ref[...] = jnp.broadcast_to((mixed / total).astype(BF16)[None], out_ref.shape)


def vision_attention(part, pitch, copies, ends, query, keyval, marks):
    vmem = pl.BlockSpec(memory_space=pltpu.VMEM)
    return pl.pallas_call(
        functools.partial(vision_kernel, part, pitch),
        out_shape=jax.ShapeDtypeStruct((copies, HEAD_DIM, query.shape[0]), BF16),
        in_specs=[pl.BlockSpec(memory_space=pltpu.SMEM)] + [vmem] * 3,
        out_specs=vmem,
        compiler_params=pltpu.CompilerParams(vmem_limit_bytes=16 * 1024 * 1024),
        name="vision_attention",
    )(ends, query, keyval, marks)


def per_device(
    patches,
    vis_gain,
    vis_bias,
    vis_qkv,
    vis_qkv_bias,
    vis_out,
    vis_out_bias,
    proj_weight,
    proj_bias,
    text_embeds,
    dec_gain,
    dec_qkv,
    dec_out,
    image_tokens,
    text_gaps,
    doc_lengths,
):
    cols = lax.axis_size("col")
    rows = lax.axis_size("row")
    row = lax.axis_index("row")
    col = lax.axis_index("col")
    half = lax.axis_index("grp")

    feat_c = vis_out.shape[1]
    vis_n = vis_qkv.shape[1]
    unit = -(-(vis_n + HEAD_DIM) // 128) * 128
    packed, own_rows_out = pack_arguments(
        unit,
        cols,
        dec_qkv,
        vis_out,
        vis_qkv,
        dec_out,
        proj_weight,
        patches,
        vis_gain,
        vis_bias,
        vis_out_bias,
    )
    gathered_w = lax.all_gather(packed, "col", axis=0)

    def pair(number):
        return lax.slice_in_dim(gathered_w, 2 * number, 2 * number + 2, axis=1)

    rows_b = patches.shape[1]
    part = rows_b // cols
    mine = exchange(own_rows_out, "col")
    mine = jnp.transpose(mine, (1, 0, 2)).reshape(part + 8, WIDTH)
    affine = mine[part : part + 3].astype(F32)

    text = text_embeds[0].T
    positions = text.shape[1]
    folds = -(-(WIDTH + HEAD_DIM) // positions)
    spare = folds * positions - WIDTH
    gain = jnp.broadcast_to(jnp.pad(dec_gain, (0, spare - HEAD_DIM))[None], (part, spare))
    folded = jnp.concatenate([mine[:part], gain], axis=1)
    folded = jnp.transpose(folded.reshape(part, folds, positions), (1, 0, 2))
    both = spread(
        jnp.concatenate([text, folded.reshape(folds * part, positions)], axis=0), "row"
    )
    text_all = both[:, :HEAD_DIM].reshape(WIDTH, positions)
    raw = jnp.transpose(
        both[:, HEAD_DIM:].reshape(rows, folds, part, positions), (0, 2, 1, 3)
    ).reshape(rows, part, folds * positions)
    gain_all = raw[:, 0, WIDTH : WIDTH + HEAD_DIM].reshape(WIDTH, 1).astype(F32)
    raw = raw[:, :, :WIDTH].reshape(rows * part, WIDTH)

    row_pack, gathered_w = lax.optimization_barrier((pair(0), gathered_w))
    row_w = exchange(row_pack.reshape(rows, HEAD_DIM, unit), "row").reshape(WIDTH, unit)

    vis_w = pair(1).reshape(WIDTH, unit)
    xfull = raw.astype(F32)
    mean = jnp.sum(xfull, axis=1, keepdims=True) / WIDTH
    variance = jnp.sum(xfull * xfull, axis=1, keepdims=True) / WIDTH - mean * mean
    normed = (
        (xfull - mean) * lax.rsqrt(variance + 1e-06) * affine[0:1] + affine[1:2]
    ).astype(BF16)
    qkv_rows = (
        jnp.dot(normed, vis_w, preferred_element_type=F32)[:, :vis_n]
        + vis_qkv_bias.astype(F32)
    ).astype(BF16)
    text_all, qkv_rows = lax.optimization_barrier((text_all, qkv_rows))
    xtext = text_all.astype(F32)
    squares = jnp.sum(xtext * xtext, axis=0, keepdims=True)
    text_normed = (xtext * lax.rsqrt(squares / WIDTH + 1e-05) * gain_all).astype(BF16)
    count = rows * part
    query = qkv_rows[:, :HEAD_DIM]
    lengths, gaps = image_tokens[0], text_gaps[0]
    own_rows = col * positions + jnp.arange(positions, dtype=jnp.int32)
    source, inside = insert_map(own_rows, lengths, gaps)
    query_pos = sequence_position(own_rows, half)
    ends = running(doc_lengths)
    low = jnp.max(
        jnp.where(query_pos[:, None] >= ends[None, :], ends[None, :], 0), axis=1
    )
    merged = count // 4
    pack = part // 4
    item = jnp.arange(merged, dtype=jnp.int32)
    merged_id = item // pack * (pack * cols) + col * pack + item % pack
    marks = jnp.tile(segment_of(merged_id, lengths), 4)[None]
    image_ends = running(lengths)
    place = sequence_position(rows_of_merged(merged_id, lengths, gaps), half)
    place = jnp.stack([place // 64, place % 64], axis=1).astype(BF16)
    total_merged = cols * merged
    first = jnp.min(jnp.where(inside, source, total_merged))
    found = jnp.sum(inside.astype(jnp.int32), dtype=jnp.int32)
    rank = jnp.where(inside, source - first, -1)
    near = jnp.arange(total_merged, dtype=jnp.int32)
    row_of = first + near
    slot = (row_of // pack % cols * 2 + half) * merged
    slot = slot + row_of // (pack * cols) * pack + row_of % pack
    near_pos = sequence_position(rows_of_merged(row_of, lengths, gaps), half)
    near_low = jnp.max(jnp.where(near_pos[:, None] >= ends[None, :], ends[None, :], 0), axis=1)
    packed = jnp.stack([near_low, near_pos - near_low, jnp.where(near < found, slot, -1)])
    qpos = jnp.stack([low, query_pos - low, rank])
    bounds = jnp.stack([jnp.min(low) // (2 * positions), col + 1, found]).astype(jnp.int32)
    bias = jnp.where(inside, NEG, 0.0).astype(BF16)[None]
    row_w, vis_kv, qpos, bounds, marks, image_ends, place, packed, bias = (
        lax.optimization_barrier(
            (
                row_w,
                qkv_rows[:, HEAD_DIM:],
                qpos,
                bounds,
                marks,
                image_ends,
                place,
                packed,
                bias,
            )
        )
    )
    keyval = spread(vis_kv, "col").reshape(cols * count, 2 * HEAD_DIM)
    proj_w = pair(2).reshape(WIDTH, unit)
    dec_out_w = vis_w[:, vis_n : vis_n + HEAD_DIM]

    text_qkv = dot0(row_w, text_normed)[:vis_n].astype(BF16)
    own_kv = jnp.concatenate(
        [
            text_qkv[HEAD_DIM : 2 * HEAD_DIM],
            jnp.pad(bias, ((0, 7), (0, 0))),
            text_qkv[2 * HEAD_DIM :],
        ],
        axis=0,
    )
    other_kv = lax.ppermute(own_kv, "grp", [(0, 1), (1, 0)])
    pair_kv = jnp.where(half == 0, jnp.stack([own_kv, other_kv]), jnp.stack([other_kv, own_kv]))
    pair_kv, keyval = lax.optimization_barrier((pair_kv, keyval))
    all_kv = lax.all_gather(pair_kv, "col", axis=0)

    def window_first(array):
        features = array.shape[1]
        return jnp.transpose(
            array.reshape(rows, part // 4, 4, features), (2, 0, 1, 3)
        ).reshape(count, features)

    query = jnp.pad(window_first(query), ((0, 0), (0, HEAD_DIM)))
    all_attn = exchange(
        vision_attention(part, rows_b, rows, image_ends, query, keyval, marks), "row"
    ).reshape(WIDTH, count)
    raw_at = row * HEAD_DIM
    own_raw = window_first(lax.dynamic_slice(raw, (0, raw_at), (count, HEAD_DIM)))
    own_bias = lax.dynamic_slice(affine[2], (raw_at,), (HEAD_DIM,))
    resid = (own_raw.T.astype(F32) + dot0(row_w, all_attn)[vis_n : vis_n + HEAD_DIM] + own_bias[:, None]).astype(BF16)
    all_resid = spread(resid, "row").reshape(WIDTH, count)
    windows = dot0(proj_w, all_resid)
    projected = proj_bias.astype(F32)[:, None]
    for window in range(4):
        projected = projected + windows[
            window * HEAD_DIM : (window + 1) * HEAD_DIM, window * merged : (window + 1) * merged
        ]
    image_in = projected.T.astype(BF16)

    image_all = jnp.transpose(spread(image_in, "row"), (1, 0, 2)).reshape(merged, WIDTH)
    ximage = image_all.astype(F32)
    squares = jnp.sum(ximage * ximage, axis=1, keepdims=True)
    image_normed = (
        ximage * lax.rsqrt(squares / WIDTH + 1e-05) * gain_all[:, 0][None, :]
    ).astype(BF16)
    all_kv, image_normed = lax.optimization_barrier((all_kv, image_normed))
    image_qkv = jnp.dot(image_normed, row_w, preferred_element_type=F32)[:, :vis_n].astype(BF16)

    def with_mask_row(query):
        return jnp.concatenate(
            [query, jnp.ones((1, positions), BF16), jnp.zeros((7, positions), BF16)], axis=0
        )

    text_query = with_mask_row(text_qkv[:HEAD_DIM])
    mixed, stats = text_attention(bounds, text_query, all_kv, qpos)
    shared = spread(
        jnp.concatenate(
            [
                image_qkv[:, : 2 * HEAD_DIM],
                jnp.zeros((merged, 8), BF16),
                image_qkv[:, 2 * HEAD_DIM :],
                image_in,
                place,
            ],
            axis=1,
        ),
        ("col", "grp"),
    )
    shared, mixed = lax.optimization_barrier((shared, mixed))
    shared = shared.reshape(cols * 2 * merged, -1)
    dec_attn, dec_input = image_attention(
        bounds, shared, text, text_query, all_kv, qpos, packed, mixed, stats
    )

    all_dec = spread(dec_attn, "row").reshape(WIDTH, positions)
    delta = dot0(dec_out_w, all_dec)
    return (dec_input.astype(F32) + delta).astype(BF16).T[None]


def solution(mesh):
    return jax.shard_map(
        per_device,
        mesh=mesh,
        in_specs=(
            P("grp", "row", "col"),
            P("col"),
            P("col"),
            P("col", "row"),
            P("row"),
            P("row", "col"),
            P("col"),
            P(None, "col", "row"),
            P("row"),
            P("grp", "col", "row"),
            P("row"),
            P("row", "col"),
            P("col", "row"),
            P("grp", None),
            P("grp", None),
            P(),
        ),
        out_specs=P("grp", "col", "row"),
        check_vma=False,
    )
```
